512 devices in a mesh: segment: 4 (over y), shard: 16 (over z), stream: 8 (over x, core).
Axes of the slice: x: 4, y: 4, z: 16, core: 2. Of those that a mesh axis runs over, the one named last changes fastest.
Arguments:
- latents: bfloat16 [32, 16, 16, 32, 256], P('stream', 'shard'), parts along dimension 0, may hold values from -6 to 6
- norm_gain: float32 [4, 256], P('segment'), may hold values from 0.25 to 1.75
- time_weight: bfloat16 [4, 3, 256, 256], P('segment'), may hold values from -0.21875 to 0.21875
- space_weight: bfloat16 [4, 9, 256, 256], P('segment'), may hold values from -0.125 to 0.125
- carry_in: bfloat16 [4, 16, 16, 32, 256], P('segment', 'stream', 'shard'), parts along dimension 1, may hold values from -6 to 6
Outputs:
- decoded: bfloat16 [32, 16, 16, 32, 256], P(('stream', 'segment'), 'shard'), parts along dimension 0
- carry_out: bfloat16 [4, 16, 16, 32, 256], P('segment', 'stream', 'shard'), parts along dimension 1
The draws below stay inside these ranges and needn't reach their ends.
There are 8 independent parts, one for each index of `stream`. The reference program is written for one: setup_inputs(seed, part) draws one part's arguments, and reference() takes and returns one part's arrays. A program takes and returns all parts, laid end to end along the dimension named above; an argument that names none is the same for every part. Nothing has to cross between parts.
All inputs are finite; a program needn't handle non-finite values.
Results may differ from the reference program's by a relative error of at most 0.009.
Values may be sent and summed in bfloat16 or wider, within the bound.
No kernel may reach another device: no remote copies, remote signals or barrier semaphores. Data moves between devices by JAX's collectives and lax.ppermute only.
A program may use at most 64 MiB of HBM per device.

```python
import jax
import jax.numpy as jnp
from jax import lax

C = 256
W = 32
SECTIONS = 4
BLOCKS = 4
FRAMES = 16
H = 16


def level_of(key, shape, split, smallest, largest):
    gain, own = 1.0, jax.random.fold_in(key, 6)
    for dim, blocks in split:
        steps = jnp.exp(jax.random.uniform(jax.random.fold_in(own, dim), (blocks,), jnp.float32, smallest / len(split), largest / len(split)))
        gain = gain * jnp.repeat(steps, shape[dim] // blocks).reshape([-1 if axis == dim else 1 for axis in range(len(shape))])
    return gain


def bell_draw(key, shape, scale, bound, split=(), kind=jnp.bfloat16):
    entries = jax.random.normal(key, shape, jnp.float32) * scale
    if len(split) > 0:
        entries = level_of(key, shape, split, -0.22, 0.18) * entries
    return jnp.clip(entries, min=-bound, max=bound).astype(kind)


def setup_inputs(seed: int = 0, part: int = 0) -> dict:
    keys = jax.random.split(jax.random.key(seed), 6)
    part_splits = jax.random.split(jax.random.fold_in(keys[5], part), 6)
    latents = bell_draw(part_splits[0], (BLOCKS, FRAMES, H, W, C), 1.0, 6.0, ((1, 16),))
    norm_gain = jnp.clip(1.0 + 0.15 * jax.random.normal(keys[1], (SECTIONS, C), jnp.float32), 0.25, 1.75)
    time_weight = bell_draw(keys[2], (SECTIONS, 3, C, C), (3 * C) ** -0.5, 0.21875, ((0, 4),))
    space_weight = bell_draw(keys[3], (SECTIONS, 9, C, C), (9 * C) ** -0.5, 0.125, ((0, 4),))
    carry_in = bell_draw(part_splits[4], (SECTIONS, 2, H, W, C), 1.0, 6.0, ((0, 4), (2, 16)))
    return dict(latents=latents, norm_gain=norm_gain, time_weight=time_weight, space_weight=space_weight, carry_in=carry_in)


def normalize(frames_in, gain_row):
    values = frames_in.astype(jnp.float32)
    inverse = jax.lax.rsqrt(lax.optimization_barrier(jnp.mean(values * values, axis=-1, keepdims=True)) + 1e-06)
    return (values * inverse * gain_row).astype(jnp.bfloat16)

def project(frames_in, matrix):
    channels = frames_in.shape[-1]
    product = jnp.dot(frames_in.reshape(-1, channels), matrix, preferred_element_type=jnp.float32)
    return product.reshape(frames_in.shape[:-1] + (matrix.shape[1],))

def spatial(hidden, kernel):
    padded = jnp.pad(hidden, ((0, 0), (1, 1), (1, 1), (0, 0)))
    height = hidden.shape[1]
    across = hidden.shape[2]
    summed = jnp.zeros(hidden.shape, jnp.float32)
    for offset in range(9):
        row_shift = offset // 3
        col_shift = offset % 3
        summed = summed + project(padded[:, row_shift:row_shift + height, col_shift:col_shift + across], kernel[offset])
    return summed

def reference(latents, norm_gain, time_weight, space_weight, carry_in):
    carries = [carry_in[section] for section in range(SECTIONS)]
    outputs = []
    for which_block in range(BLOCKS):
        current = latents[which_block]
        for section in range(SECTIONS):
            normed = normalize(current, norm_gain[section])
            extended = jnp.concatenate([carries[section], normed], axis=0)
            mixed = project(extended[0:FRAMES], time_weight[section, 0])
            mixed = mixed + project(extended[1:FRAMES + 1], time_weight[section, 1])
            mixed = mixed + project(extended[2:FRAMES + 2], time_weight[section, 2])
            hidden = jax.nn.silu(mixed).astype(jnp.bfloat16)
            carries[section] = normed[FRAMES - 2:]
            current = (current.astype(jnp.float32) + spatial(hidden, space_weight[section])).astype(jnp.bfloat16)
        outputs.append(current)
    return (jnp.stack(outputs), jnp.stack(carries))
```

```python
import functools

import jax
import jax.numpy as jnp
from jax import lax
from jax.experimental import pallas as pl
from jax.experimental.pallas import tpu as pltpu
from jax.sharding import PartitionSpec as P


C = 256
LANES = 128
HALF = 128
TAPS = 12
GAIN_ROW = TAPS * HALF
PACKED = GAIN_ROW + 16
FRAMES = 16
SECTIONS = 4
F32 = jnp.float32
BF16 = jnp.bfloat16

VMEM = pl.BlockSpec(memory_space=pltpu.VMEM)
ANY = pl.BlockSpec(memory_space=pl.ANY)
SMEM = pl.BlockSpec(memory_space=pltpu.SMEM)


def shape_of(*dims, dtype=BF16):
    return jax.ShapeDtypeStruct(dims, dtype)


def call(kernel, name, outs, in_specs, scratch=(), flops=1 << 20, moved=1 << 20):
    out_specs = tuple(VMEM for _ in outs) if isinstance(outs, tuple) else VMEM
    return pl.pallas_call(
        kernel,
        out_shape=outs,
        in_specs=in_specs,
        out_specs=out_specs,
        scratch_shapes=list(scratch),
        name=name,
        cost_estimate=pl.CostEstimate(flops=flops, bytes_accessed=moved, transcendentals=0),
        compiler_params=pltpu.CompilerParams(vmem_limit_bytes=16 << 20),
    )


def chunk_kernel(columns, row, out):
    flat = columns[...].reshape(16, 32, C)
    for side in range(2):
        lanes = slice(side * LANES, (side + 1) * LANES)
        out[:, side * 32 : side * 32 + 32, :] = flat[:, :, lanes]
        for frame in range(2):
            at = 64 + 4 * side + 2 * frame
            for z in range(16):
                out[z, at : at + 2, :] = row[frame, 2 * z : 2 * z + 2, lanes]


def pack_kernel(scal, gain, taps_time, taps_space, out, sems):
    at = pl.multiple_of(scal[1] * HALF, HALF)
    copies = []
    for tap in range(TAPS):
        own = taps_time.at[0, tap] if tap < 3 else taps_space.at[0, tap - 3]
        copies.append(
            pltpu.make_async_copy(own.at[pl.ds(at, HALF)], out.at[pl.ds(tap * HALF, HALF)], sems.at[tap])
        )
        copies[-1].start()
    value = gain[...]
    high = value.astype(BF16)
    rest = value - high.astype(F32)
    middle = rest.astype(BF16)
    low = (rest - middle.astype(F32)).astype(BF16)
    pick = lax.broadcasted_iota(jnp.int32, (16, C), 0)
    rows = jnp.where(pick == 0, high.astype(F32), 0.0)
    rows = jnp.where(pick == 1, middle.astype(F32), rows)
    rows = jnp.where(pick == 2, low.astype(F32), rows)
    for copy in copies:
        copy.wait()
    out[GAIN_ROW:PACKED, :] = rows.astype(BF16)


def unpack_kernel(got, frames, before, carry):
    for side in range(2):
        lanes = slice(side * LANES, (side + 1) * LANES)
        block = got[:, side * 32 : side * 32 + 32, :]
        frames[:, :, lanes] = block
        before[:, :, lanes] = block[8:16]
        for n in range(4):
            frame, col = n // 2, n % 2
            carry[frame, col * 16 : col * 16 + 16, lanes] = got[:, 64 + 4 * side + n, :]


def weights_kernel(section, scal, gain, taps_time, taps_space, *rest):
    bufs, (_, out, gain_out, terms, sems, gain_sem) = rest[:6], rest[6:]
    mine, core = scal[0], scal[1]
    rel = lax.rem(section - mine + SECTIONS, SECTIONS)
    plan = []
    for tap in range(TAPS):
        for side in range(2):
            at = pl.multiple_of((core if side == 0 else 1 - core) * HALF, HALF)
            plan.append((tap, side, at, out.at[tap, pl.ds(at, HALF)]))

    @pl.when(rel == 0)
    def _():
        for tap, side, at, dst in plan:
            own = taps_time.at[0, tap] if tap < 3 else taps_space.at[0, tap - 3]
            pltpu.make_async_copy(own.at[pl.ds(at, HALF)], dst, sems.at[tap, side]).start()
        pltpu.make_async_copy(bufs[0].at[pl.ds(GAIN_ROW, 16)], terms, gain_sem).start()

    for which in range(3):

        @pl.when(rel == which + 1)
        def _(which=which):
            for tap, side, at, dst in plan:
                src = bufs[2 * which + side].at[pl.ds(tap * HALF, HALF)]
                pltpu.make_async_copy(src, dst, sems.at[tap, side]).start()
            pltpu.make_async_copy(bufs[2 * which].at[pl.ds(GAIN_ROW, 16)], terms, gain_sem).start()

    pltpu.make_async_copy(bufs[0].at[pl.ds(GAIN_ROW, 16)], terms, gain_sem).wait()
    rows = terms[...].astype(F32)
    received = rows[0:1] + (rows[1:2] + rows[2:3])
    gain_out[...] = jnp.where(rel == 0, gain[...], received)
    for tap, side, at, dst in plan:
        pltpu.make_async_copy(bufs[side].at[pl.ds(tap * HALF, HALF)], dst, sems.at[tap, side]).wait()


def weights_call(section, scal, gain, taps_time, taps_space, bufs, after):
    return call(
        functools.partial(weights_kernel, section),
        "weights",
        (shape_of(TAPS, C, C), shape_of(1, C, dtype=F32)),
        [SMEM, VMEM] + [ANY] * 9,
        [pltpu.VMEM((16, C), BF16), pltpu.SemaphoreType.DMA((TAPS, 2)), pltpu.SemaphoreType.DMA],
        moved=3 << 20,
    )(scal, gain, taps_time, taps_space, *bufs, after)


def normed_of(values, gain_row):
    inverse = lax.rsqrt(jnp.mean(values * values, axis=-1, keepdims=True) + 1e-06)
    return (values * inverse * gain_row).astype(BF16)


def pieces(count, size):
    return [(at, min(size, count - at)) for at in range(0, count, size)]


def mix(source, weights, left, right, count):
    taps = weights[0:3].reshape(3 * C, C)
    for at, size in pieces(count, 8):
        parts = [source[at + k : at + k + size].reshape(size * 32, C) for k in range(3)]
        mixed = jnp.dot(jnp.concatenate(parts, axis=-1), taps, preferred_element_type=F32)
        hidden = jax.nn.silu(mixed).astype(BF16).reshape(size, 32, C)
        left[at : at + size] = hidden[:, 0:16, :]
        right[at : at + size] = hidden[:, 16:32, :]


def first_time_kernel(scal, frames, before, carry, gain, weights, left, right, tail, normed):
    row = gain[...]
    for source, start, count in ((before, 0, 8), (frames, 8, 16)):
        for at, size in pieces(count, 8):
            values = source[at : at + size].astype(F32).reshape(size * 32, C)
            normed[start + at : start + at + size] = normed_of(values, row).reshape(size, 32, C)
    tail[...] = normed[22:24]

    @pl.when(scal[0] == 0)
    def _():
        normed[6:8] = carry[...]

    mix(normed, weights, left, right, 22)


def time_kernel(count, normed, weights, left, right):
    mix(normed, weights, left, right, count)


def first_time_call(scal, frames, before, carry, gain, weights):
    return call(
        first_time_kernel,
        "first_time",
        (shape_of(22, 16, C), shape_of(22, 16, C), shape_of(2, 32, C)),
        [SMEM] + [VMEM] * 5,
        [pltpu.VMEM((24, 32, C), BF16)],
        flops=1 << 28,
    )(scal, frames, before, carry, gain, weights)


def time_call(count, normed, weights):
    return call(
        functools.partial(time_kernel, count),
        "time",
        (shape_of(count, 16, C), shape_of(count, 16, C)),
        [VMEM] * 2,
        flops=1 << 28,
    )(normed, weights)


def spread(y, row):
    down = jnp.where(row == 0, 0.0, pltpu.roll(y[0], 1, 0))
    up = jnp.where(row == 15, 0.0, pltpu.roll(y[2], y[2].shape[0] - 1, 0))
    return y[1] + down + up


def inner_kernel(count, left, right, weights, acc):
    size = count * 16
    row = lax.broadcasted_iota(jnp.int32, (size, C), 0) % 16
    lhs = jnp.concatenate([left[...].reshape(size, C), right[...].reshape(size, C)], axis=-1)
    for col in range(2):
        y = []
        for p in range(3):
            tap = 3 + 3 * p + 1 - col
            y.append(jnp.dot(lhs, weights[tap : tap + 2].reshape(2 * C, C), preferred_element_type=F32))
        acc[:, col * 16 : col * 16 + 16, :] = spread(y, row).reshape(count, 16, C)


def inner_call(count, left, right, weights):
    return call(
        functools.partial(inner_kernel, count),
        "inner",
        shape_of(count, 32, C, dtype=F32),
        [VMEM] * 3,
        flops=1 << 29,
    )(left, right, weights)


def edge_result(count, col, acc, came_left, came_right, weights, row):
    size = count * 16
    lhs = (came_left if col == 0 else came_right)[...].reshape(size, C)
    y = [jnp.dot(lhs, weights[3 + 3 * p + 2 * col], preferred_element_type=F32) for p in range(3)]
    at = slice(col * 16, col * 16 + 16)
    return spread(y, row) + acc[:, at, :].reshape(size, C)


def edge_kernel(count, scal, acc, came_left, came_right, weights, kept, gain, *rest):
    held, (out, normed, tail) = rest[:-3], rest[-3:]
    row = lax.broadcasted_iota(jnp.int32, (count * 16, C), 0) % 16
    for col in range(2):
        at = slice(col * 16, col * 16 + 16)
        total = edge_result(count, col, acc, came_left, came_right, weights, row)
        if len(held) == 2:
            a = jnp.concatenate([held[0][2:8, at, :], held[1][:, at, :]], axis=0)
        else:
            a = held[0][2:, at, :]
        result = (a.reshape(count * 16, C).astype(F32) + total).astype(BF16)
        out[:, at, :] = result.reshape(count, 16, C)
        n = normed_of(result.astype(F32), gain[...]).reshape(count, 16, C)
        normed[:, at, :] = n
        tail[:, at, :] = n[count - 2 : count]

    @pl.when(scal[0] == 0)
    def _():
        normed[count - 18 : count - 16] = kept[...]


def edge_call(count, scal, acc, came_left, came_right, weights, kept, gain, held):
    return call(
        functools.partial(edge_kernel, count),
        "edge",
        (shape_of(count, 32, C), shape_of(count, 32, C), shape_of(2, 32, C)),
        [SMEM] + [VMEM] * (6 + len(held)),
        flops=1 << 28,
    )(scal, acc, came_left, came_right, weights, kept, gain, *held)


def last_edge_kernel(acc, came_left, came_right, weights, held, carry, out):
    row = lax.broadcasted_iota(jnp.int32, (FRAMES * 16, C), 0) % 16
    for col in range(2):
        at = slice(col * 16, col * 16 + 16)
        total = edge_result(FRAMES, col, acc, came_left, came_right, weights, row)
        a = held[2:, at, :].reshape(FRAMES * 16, C)
        result = (a.astype(F32) + total).astype(BF16).reshape(FRAMES, 16, C)
        for side in range(2):
            lanes = slice(side * LANES, (side + 1) * LANES)
            to = side * 32 + col * 16
            out[:, to : to + 16, :] = result[:, :, lanes]
    for side in range(2):
        lanes = slice(side * LANES, (side + 1) * LANES)
        for n in range(4):
            frame, col = n // 2, n % 2
            out[:, 64 + 4 * side + n, :] = carry[frame, col * 16 : col * 16 + 16, lanes]


def last_edge_call(acc, came_left, came_right, weights, held, carry):
    return call(
        last_edge_kernel,
        "last_edge",
        shape_of(16, 72, LANES),
        [VMEM] * 6,
        flops=1 << 28,
    )(acc, came_left, came_right, weights, held, carry)


def body(latents, norm_gain, time_weight, space_weight, carry_in):
    shards = lax.axis_size("shard")
    streams = lax.axis_size("stream")
    mine = lax.axis_index("segment")
    core = lax.rem(lax.axis_index("stream"), 2)
    scal = jnp.stack([mine, core]).astype(jnp.int32)

    def ring(distance):
        return [(i, (i + distance) % SECTIONS) for i in range(SECTIONS)]

    def over_segments(array, pairs):
        return lax.ppermute(array, "segment", pairs)

    swap = [(i, i ^ 1) for i in range(streams)]
    up = [(i, i + 1) for i in range(shards - 1)]
    down = [(i + 1, i) for i in range(shards - 1)]

    block = lax.dynamic_index_in_dim(latents, mine, 0, keepdims=False)[0]
    chunks = call(chunk_kernel, "chunk", shape_of(16, 72, LANES), [VMEM] * 2)(
        block.transpose(1, 0, 2), carry_in[0, :, 0]
    )
    with jax.named_scope("turn"):
        got = lax.all_to_all(chunks, "shard", split_axis=0, concat_axis=0, tiled=True)

    packed = call(
        pack_kernel,
        "pack",
        shape_of(PACKED, C),
        [SMEM, VMEM, ANY, ANY],
        [pltpu.SemaphoreType.DMA((TAPS,))],
    )(scal, norm_gain, time_weight, space_weight)
    bufs = []
    for distance in (-1, 2, 1):
        with jax.named_scope("spread"):
            buf = over_segments(packed, ring(distance))
        with jax.named_scope("swap"):
            bufs += [buf, lax.ppermute(buf, "stream", swap)]

    frames, sent_before, carry = call(
        unpack_kernel,
        "unpack",
        (shape_of(16, 32, C), shape_of(8, 32, C), shape_of(2, 32, C)),
        [VMEM],
    )(got)
    before = over_segments(sent_before, [(0, 1), (1, 2), (2, 3)])
    near = over_segments(carry, [(1, 0), (3, 2)])
    far = over_segments(jnp.concatenate([carry, near], axis=0), [(2, 0)])
    kept = (carry, near, far[0:2], far[2:4])

    weights, gain = weights_call(0, scal, norm_gain, time_weight, space_weight, bufs, before)
    left, right, tail = first_time_call(scal, frames, before, carry, gain, weights)
    tails = [tail]
    held = (before, frames)
    for section in range(SECTIONS):
        count = FRAMES + 2 * (SECTIONS - 1 - section)
        if section > 0:
            left, right = time_call(count, normed, weights)
        came_right = lax.ppermute(left, "shard", down)
        came_left = lax.ppermute(right, "shard", up)
        acc = inner_call(count, left, right, weights)
        if section == 2:
            over = over_segments(jnp.concatenate([tails[1], tails[2]], axis=0), [(3, 2)])
        if section == 3:
            wrapped = over_segments(jnp.where(mine == 3, tails[0], over[0:2]), [(3, 0), (2, 1)])
            carry = jnp.where(mine == 3, tails[3], jnp.where(mine == 2, over[2:4], wrapped))
            out = last_edge_call(acc, came_left, came_right, weights, held[0], carry)
        else:
            following, gain = weights_call(
                section + 1, scal, norm_gain, time_weight, space_weight, bufs, left
            )
            a, normed, tail = edge_call(
                count, scal, acc, came_left, came_right, weights, kept[section + 1], gain, held
            )
            held = (a,)
            tails.append(tail)
            weights = following
    sent = lax.all_to_all(out, "shard", split_axis=0, concat_axis=0, tiled=True)
    main = jnp.concatenate([sent[:, 0:32], sent[:, 32:64]], axis=-1)
    decoded = main.reshape(32, 16, C).transpose(1, 0, 2)[None, None]
    kept_rows = jnp.concatenate([sent[:, 64:68], sent[:, 68:72]], axis=-1)
    carry_out = kept_rows.reshape(shards, 2, 2, C).transpose(1, 0, 2, 3).reshape(1, 2, 1, 32, C)
    return (decoded, carry_out)


def solution(mesh):
    placed = (
        P("stream", "shard", None, None, None),
        P("segment", None),
        P("segment", None, None, None),
        P("segment", None, None, None),
        P("segment", "stream", "shard", None, None),
    )
    return jax.shard_map(
        body,
        mesh=mesh,
        in_specs=placed,
        out_specs=(
            P(("stream", "segment"), "shard", None, None, None),
            P("segment", "stream", "shard", None, None),
        ),
        check_vma=False,
    )
```

```python
import functools

import jax
import jax.numpy as jnp
from jax import lax
from jax.experimental import pallas as pl
from jax.experimental.pallas import tpu as pltpu
from jax.sharding import PartitionSpec as P


C = 256
LANES = 128
HALF = 128
TAPS = 12
GAIN_ROW = TAPS * HALF
PACKED = GAIN_ROW + 16
FRAMES = 16
SECTIONS = 4
F32 = jnp.float32
BF16 = jnp.bfloat16

VMEM = pl.BlockSpec(memory_space=pltpu.VMEM)
ANY = pl.BlockSpec(memory_space=pl.ANY)
SMEM = pl.BlockSpec(memory_space=pltpu.SMEM)


def shape_of(*dims, dtype=BF16):
    return jax.ShapeDtypeStruct(dims, dtype)


def call(kernel, name, outs, in_specs, scratch=(), flops=1 << 20, moved=1 << 20):
    out_specs = tuple(VMEM for _ in outs) if isinstance(outs, tuple) else VMEM
    return pl.pallas_call(
        kernel,
        out_shape=outs,
        in_specs=in_specs,
        out_specs=out_specs,
        scratch_shapes=list(scratch),
        name=name,
        cost_estimate=pl.CostEstimate(flops=flops, bytes_accessed=moved, transcendentals=0),
        compiler_params=pltpu.CompilerParams(vmem_limit_bytes=20 << 20),
    )


def chunk_kernel(columns, row, out):
    flat = columns[...].reshape(16, 32, C)
    for side in range(2):
        lanes = slice(side * LANES, (side + 1) * LANES)
        out[:, side * 32 : side * 32 + 32, :] = flat[:, :, lanes]
        for frame in range(2):
            at = 64 + 4 * side + 2 * frame
            for z in range(16):
                out[z, at : at + 2, :] = row[frame, 2 * z : 2 * z + 2, lanes]


def pack_kernel(scal, gain, taps_time, taps_space, out, sems):
    at = pl.multiple_of(scal[1] * HALF, HALF)
    copies = []
    for tap in range(TAPS):
        own = taps_time.at[0, tap] if tap < 3 else taps_space.at[0, tap - 3]
        copies.append(
            pltpu.make_async_copy(own.at[pl.ds(at, HALF)], out.at[pl.ds(tap * HALF, HALF)], sems.at[tap])
        )
        copies[-1].start()
    value = gain[...]
    high = value.astype(BF16)
    rest = value - high.astype(F32)
    middle = rest.astype(BF16)
    low = (rest - middle.astype(F32)).astype(BF16)
    pick = lax.broadcasted_iota(jnp.int32, (16, C), 0)
    rows = jnp.where(pick == 0, high.astype(F32), 0.0)
    rows = jnp.where(pick == 1, middle.astype(F32), rows)
    rows = jnp.where(pick == 2, low.astype(F32), rows)
    for copy in copies:
        copy.wait()
    out[GAIN_ROW:PACKED, :] = rows.astype(BF16)


def unpack_kernel(got, frames, before, carry):
    for side in range(2):
        lanes = slice(side * LANES, (side + 1) * LANES)
        block = got[:, side * 32 : side * 32 + 32, :]
        frames[:, :, lanes] = block
        before[:, :, lanes] = block[8:16]
        for n in range(4):
            frame, col = n // 2, n % 2
            carry[frame, col * 16 : col * 16 + 16, lanes] = got[:, 64 + 4 * side + n, :]


def fetch(section, scal, own, bufs, out, terms, sems, gain_sem):
    mine, core = scal[0], scal[1]
    rel = lax.rem(section - mine + SECTIONS, SECTIONS)
    plan = []
    for tap in range(TAPS):
        for side in range(2):
            at = pl.multiple_of((core if side == 0 else 1 - core) * HALF, HALF)
            plan.append((tap, side, at, out.at[tap, pl.ds(at, HALF)]))
    taps_time, taps_space = own

    @pl.when(rel == 0)
    def _():
        for tap, side, at, dst in plan:
            src = taps_time.at[0, tap] if tap < 3 else taps_space.at[0, tap - 3]
            pltpu.make_async_copy(src.at[pl.ds(at, HALF)], dst, sems.at[tap, side]).start()
        pltpu.make_async_copy(bufs[0].at[pl.ds(GAIN_ROW, 16)], terms, gain_sem).start()

    for which in range(3):

        @pl.when(rel == which + 1)
        def _(which=which):
            for tap, side, at, dst in plan:
                src = bufs[2 * which + side].at[pl.ds(tap * HALF, HALF)]
                pltpu.make_async_copy(src, dst, sems.at[tap, side]).start()
            pltpu.make_async_copy(bufs[2 * which].at[pl.ds(GAIN_ROW, 16)], terms, gain_sem).start()

    def wait(first, last):
        for tap, side, at, dst in plan:
            if first <= tap < last:
                pltpu.make_async_copy(
                    bufs[side].at[pl.ds(tap * HALF, HALF)], dst, sems.at[tap, side]
                ).wait()

    def gain_row(gain):
        pltpu.make_async_copy(bufs[0].at[pl.ds(GAIN_ROW, 16)], terms, gain_sem).wait()
        rows = terms[...].astype(F32)
        received = rows[0:1] + (rows[1:2] + rows[2:3])
        return jnp.where(rel == 0, gain[...], received)

    return wait, gain_row


def normed_of(values, gain_row):
    inverse = lax.rsqrt(jnp.mean(values * values, axis=-1, keepdims=True) + 1e-06)
    return (values * inverse * gain_row).astype(BF16)


def pieces(count, size):
    return [(at, min(size, count - at)) for at in range(0, count, size)]


def mix(source, weights, hidden, count, columns):
    taps = weights[0:3].reshape(3 * C, C)
    rows = columns * 16
    for at, size in pieces(count, 4):
        parts = [source[at + k : at + k + size, 0:rows].reshape(size * rows, C) for k in range(3)]
        mixed = jnp.dot(jnp.concatenate(parts, axis=-1), taps, preferred_element_type=F32)
        value = jax.nn.silu(mixed).astype(BF16).reshape(size, rows, C)
        for col in range(columns):
            hidden[col, at : at + size] = value[:, col * 16 : col * 16 + 16, :]


def spatial(hidden, weights, col, count):
    size = count * 16
    row = lax.broadcasted_iota(jnp.int32, (size, C), 0) % 16
    lhs = jnp.concatenate([hidden[col + q, 0:count].reshape(size, C) for q in range(3)], axis=-1)
    y = []
    for p in range(3):
        taps = weights[3 + 3 * p : 6 + 3 * p].reshape(3 * C, C)
        y.append(jnp.dot(lhs, taps, preferred_element_type=F32))
    down = jnp.where(row == 0, 0.0, pltpu.roll(y[0], 1, 0))
    up = jnp.where(row == 15, 0.0, pltpu.roll(y[2], size - 1, 0))
    return y[1] + down + up


def cols(col):
    return slice(col * 16, col * 16 + 16)


def pair_kernel(first, scal, gain, far, mid, left, right, *rest):
    if first:
        refs, (out, tails) = rest[:8], rest[8:10]
    else:
        refs, (out,) = rest[:8], rest[8:9]
    own, bufs = refs[:2], refs[2:]
    weights, terms, sems, gain_sem, normed, hidden, second, normed2 = rest[(10 if first else 9) :]
    section = 0 if first else 2
    total = 24 if first else 20
    mine, shard, shards = scal[0], scal[2], scal[3]
    loads = []
    for k in range(2):
        loads.append(
            fetch(section + k, scal, own, bufs, weights.at[k], terms.at[k], sems.at[k], gain_sem.at[k])
        )
    if first:
        mine_rel = lax.rem(2 - mine + SECTIONS, SECTIONS)
        for which in range(3):

            @pl.when(lax.rem(mine_rel + 2, 3) == which)
            def _(which=which):
                pltpu.make_async_copy(
                    bufs[2 * which].at[pl.ds(GAIN_ROW, 16)], terms.at[2], gain_sem.at[2]
                ).start()

    row = loads[0][1](gain)
    sources = (left, mid, right)
    for n, source in enumerate(sources):
        for at, size in pieces(total, 8):
            values = source[at : at + size].astype(F32).reshape(size * 32, C)
            normed[at : at + size, n * 32 : n * 32 + 32] = normed_of(values, row).reshape(size, 32, C)
    if first:
        tails[0] = normed[total - 2 : total, 32:64]

    @pl.when(mine == 0)
    def _():
        for n, source in enumerate(sources):
            normed[total - 18 : total - 16, n * 32 : n * 32 + 32] = source[total - 18 : total - 16]

    loads[0][0](0, 3)
    count = total - 2
    mix(normed, weights.at[0], hidden, count, 6)
    loads[0][0](3, TAPS)
    row = loads[1][1](gain)
    for col in range(4):
        source, at = ((left, cols(1)), (mid, cols(0)), (mid, cols(1)), (right, cols(0)))[col]
        a = source[2:, at, :].reshape(count * 16, C).astype(F32)
        result = (a + spatial(hidden, weights.at[0], col, count)).astype(BF16)
        if col in (1, 2):
            second[:, cols(col - 1), :] = result.reshape(count, 16, C)
        n = normed_of(result.astype(F32), row)
        if col == 0:
            n = jnp.where(shard == 0, jnp.zeros_like(n), n)
        if col == 3:
            n = jnp.where(shard == shards - 1, jnp.zeros_like(n), n)
        normed2[:, cols(col), :] = n.reshape(count, 16, C)
    own_tail = normed2[count - 2 : count, 16:48]
    if first:
        tails[1] = own_tail

    @pl.when(mine == 0)
    def _():
        for col in range(4):
            source, at = ((left, cols(1)), (mid, cols(0)), (mid, cols(1)), (right, cols(0)))[col]
            normed2[count - 18 : count - 16, cols(col)] = source[total - 20 : total - 18, at, :]

    loads[1][0](0, 3)
    count = total - 4
    mix(normed2, weights.at[1], hidden, count, 4)
    loads[1][0](3, TAPS)
    for col in range(2):
        a = second[2:, cols(col), :].reshape(count * 16, C).astype(F32)
        result = (a + spatial(hidden, weights.at[1], col, count)).astype(BF16).reshape(count, 16, C)
        if first:
            out[:, cols(col), :] = result
        else:
            for side in range(2):
                lanes = slice(side * LANES, (side + 1) * LANES)
                out[:, side * 32 + col * 16 : side * 32 + col * 16 + 16, :] = result[:, :, lanes]
    if first:
        pltpu.make_async_copy(bufs[0].at[pl.ds(GAIN_ROW, 16)], terms.at[2], gain_sem.at[2]).wait()
        rows = terms[2].astype(F32)
        received = rows[0:1] + (rows[1:2] + rows[2:3])
        row = jnp.where(mine == 2, gain[...], received)
        last = out[count - 2 : count].astype(F32).reshape(64, C)
        tails[2] = normed_of(last, row).reshape(2, 32, C)

        @pl.when(mine == 0)
        def _():
            out[0:4] = far[...]

    else:
        carry = jnp.where(mine == SECTIONS - 1, own_tail, far[...])
        for side in range(2):
            lanes = slice(side * LANES, (side + 1) * LANES)
            for n in range(4):
                out[:, 64 + 4 * side + n, :] = carry[n // 2, cols(n % 2), lanes]


def pair_call(first, scal, gain, far, sources, own, bufs):
    total = 24 if first else 20
    count = total - 2
    if first:
        outs = (shape_of(20, 32, C), shape_of(3, 2, 32, C))
    else:
        outs = shape_of(16, 72, LANES)
    return call(
        functools.partial(pair_kernel, first),
        "first_pair" if first else "last_pair",
        outs,
        [SMEM] + [VMEM] * 5 + [ANY] * 8,
        [
            pltpu.VMEM((2, TAPS, C, C), BF16),
            pltpu.VMEM((3, 16, C), BF16),
            pltpu.SemaphoreType.DMA((2, TAPS, 2)),
            pltpu.SemaphoreType.DMA((3,)),
            pltpu.VMEM((total, 96, C), BF16),
            pltpu.VMEM((6, count, 16, C), BF16),
            pltpu.VMEM((count, 32, C), BF16),
            pltpu.VMEM((count, 64, C), BF16),
        ],
        flops=1 << 31,
        moved=4 << 20,
    )(scal, gain, far, *sources, *own, *bufs)


def join_kernel(scal, frames, before, near, carry, out):
    out[8:24] = frames[...]
    out[0:8] = before[...]

    @pl.when(scal[0] == 0)
    def _():
        out[4:6] = near[...]
        out[6:8] = carry[...]


def body(latents, norm_gain, time_weight, space_weight, carry_in):
    shards = lax.axis_size("shard")
    streams = lax.axis_size("stream")
    mine = lax.axis_index("segment")
    core = lax.rem(lax.axis_index("stream"), 2)
    here = lax.axis_index("shard")
    scal = jnp.stack([mine, core, here, jnp.int32(shards)]).astype(jnp.int32)

    def ring(distance):
        return [(i, (i + distance) % SECTIONS) for i in range(SECTIONS)]

    def over_segments(array, pairs):
        return lax.ppermute(array, "segment", pairs)

    swap = [(i, i ^ 1) for i in range(streams)]
    up = [(i, i + 1) for i in range(shards - 1)]
    down = [(i + 1, i) for i in range(shards - 1)]

    block = lax.dynamic_index_in_dim(latents, mine, 0, keepdims=False)[0]
    chunks = call(chunk_kernel, "chunk", shape_of(16, 72, LANES), [VMEM] * 2)(
        block.transpose(1, 0, 2), carry_in[0, :, 0]
    )
    with jax.named_scope("turn"):
        got = lax.all_to_all(chunks, "shard", split_axis=0, concat_axis=0, tiled=True)

    packed = call(
        pack_kernel,
        "pack",
        shape_of(PACKED, C),
        [SMEM, VMEM, ANY, ANY],
        [pltpu.SemaphoreType.DMA((TAPS,))],
    )(scal, norm_gain, time_weight, space_weight)
    bufs = []
    for distance in (-1, 2, 1):
        with jax.named_scope("spread"):
            buf = over_segments(packed, ring(distance))
        with jax.named_scope("swap"):
            bufs += [buf, lax.ppermute(buf, "stream", swap)]

    frames, sent_before, carry = call(
        unpack_kernel,
        "unpack",
        (shape_of(16, 32, C), shape_of(8, 32, C), shape_of(2, 32, C)),
        [VMEM],
    )(got)
    before = over_segments(sent_before, [(0, 1), (1, 2), (2, 3)])
    near = over_segments(carry, [(1, 0), (3, 2)])
    far = over_segments(jnp.concatenate([near, carry], axis=0), [(2, 0)])
    joined = call(join_kernel, "join", shape_of(24, 32, C), [SMEM] + [VMEM] * 4)(
        scal, frames, before, near, carry
    )

    def beside(array):
        came_left = lax.ppermute(array, "shard", up)
        came_right = lax.ppermute(array, "shard", down)
        return array, came_left, came_right

    own = (time_weight, space_weight)
    middle, tails = pair_call(True, scal, norm_gain, far, beside(joined), own, bufs)
    sources = beside(middle)
    over = over_segments(tails[1:3].reshape(4, 32, C), [(3, 2)])
    wrapped = over_segments(jnp.where(mine == 3, tails[0], over[0:2]), [(3, 0), (2, 1)])
    carry = jnp.where(mine == 2, over[2:4], wrapped)
    out = pair_call(False, scal, norm_gain, carry, sources, own, bufs)
    sent = lax.all_to_all(out, "shard", split_axis=0, concat_axis=0, tiled=True)
    main = jnp.concatenate([sent[:, 0:32], sent[:, 32:64]], axis=-1)
    decoded = main.reshape(32, 16, C).transpose(1, 0, 2)[None, None]
    kept_rows = jnp.concatenate([sent[:, 64:68], sent[:, 68:72]], axis=-1)
    carry_out = kept_rows.reshape(shards, 2, 2, C).transpose(1, 0, 2, 3).reshape(1, 2, 1, 32, C)
    return (decoded, carry_out)


def solution(mesh):
    placed = (
        P("stream", "shard", None, None, None),
        P("segment", None),
        P("segment", None, None, None),
        P("segment", None, None, None),
        P("segment", "stream", "shard", None, None),
    )
    return jax.shard_map(
        body,
        mesh=mesh,
        in_specs=placed,
        out_specs=(
            P(("stream", "segment"), "shard", None, None, None),
            P("segment", "stream", "shard", None, None),
        ),
        check_vma=False,
    )
```

```python
import functools

import jax
import jax.numpy as jnp
from jax import lax
from jax.experimental import pallas as pl
from jax.experimental.pallas import tpu as pltpu
from jax.sharding import PartitionSpec as P


C = 256
LANES = 128
HALF = 128
TAPS = 12
GAIN_ROW = TAPS * HALF
PACKED = GAIN_ROW + 16
SECTIONS = 4
F32 = jnp.float32
BF16 = jnp.bfloat16

VMEM = pl.BlockSpec(memory_space=pltpu.VMEM)
HBM = pl.BlockSpec(memory_space=pltpu.HBM)
SMEM = pl.BlockSpec(memory_space=pltpu.SMEM)


def shape_of(*dims, dtype=BF16):
    return jax.ShapeDtypeStruct(dims, dtype)


def call(kernel, outs, in_specs, scratch=(), flops=1 << 20, moved=1 << 20, room=16):
    out_specs = tuple(VMEM for _ in outs) if isinstance(outs, tuple) else VMEM
    return pl.pallas_call(
        kernel,
        out_shape=outs,
        in_specs=in_specs,
        out_specs=out_specs,
        scratch_shapes=list(scratch),
        cost_estimate=pl.CostEstimate(flops=flops, bytes_accessed=moved, transcendentals=0),
        compiler_params=pltpu.CompilerParams(vmem_limit_bytes=room << 20),
    )


def chunk_kernel(columns, row, out):
    flat = columns[...].reshape(16, 32, C)
    for side in range(2):
        lanes = slice(side * LANES, (side + 1) * LANES)
        out[:, side * 32 : side * 32 + 32, :] = flat[:, :, lanes]
        for frame in range(2):
            at = 64 + 4 * side + 2 * frame
            for z in range(16):
                out[z, at : at + 2, :] = row[frame, 2 * z : 2 * z + 2, lanes]


def pack_kernel(scal, gain, taps_time, taps_space, out, sems):
    at = pl.multiple_of(scal[1] * HALF, HALF)
    copies = []
    for tap in range(TAPS):
        own = taps_time.at[0, tap] if tap < 3 else taps_space.at[0, tap - 3]
        copies.append(
            pltpu.make_async_copy(own.at[pl.ds(at, HALF)], out.at[pl.ds(tap * HALF, HALF)], sems.at[tap])
        )
        copies[-1].start()
    value = gain[...]
    high = value.astype(BF16)
    rest = value - high.astype(F32)
    middle = rest.astype(BF16)
    low = (rest - middle.astype(F32)).astype(BF16)
    pick = lax.broadcasted_iota(jnp.int32, (16, C), 0)
    rows = jnp.where(pick == 0, high.astype(F32), 0.0)
    rows = jnp.where(pick == 1, middle.astype(F32), rows)
    rows = jnp.where(pick == 2, low.astype(F32), rows)
    for copy in copies:
        copy.wait()
    out[GAIN_ROW:PACKED, :] = rows.astype(BF16)


def unpack_kernel(got, frames, before, carry):
    for side in range(2):
        lanes = slice(side * LANES, (side + 1) * LANES)
        block = got[:, side * 32 : side * 32 + 32, :]
        frames[:, :, lanes] = block
        before[:, :, lanes] = block[8:16]
        for n in range(4):
            frame, col = n // 2, n % 2
            carry[frame, col * 16 : col * 16 + 16, lanes] = got[:, 64 + 4 * side + n, :]


def fetch(section, scal, own, bufs, out, terms, sems, gain_sem):
    mine, core = scal[0], scal[1]
    rel = lax.rem(section - mine + SECTIONS, SECTIONS)
    plan = []
    for tap in range(TAPS):
        for side in range(2):
            at = pl.multiple_of((core if side == 0 else 1 - core) * HALF, HALF)
            plan.append((tap, side, at, out.at[tap, pl.ds(at, HALF)]))
    taps_time, taps_space = own

    @pl.when(rel == 0)
    def _():
        for tap, side, at, dst in plan:
            src = taps_time.at[0, tap] if tap < 3 else taps_space.at[0, tap - 3]
            pltpu.make_async_copy(src.at[pl.ds(at, HALF)], dst, sems.at[tap, side]).start()
        pltpu.make_async_copy(bufs[0].at[pl.ds(GAIN_ROW, 16)], terms, gain_sem).start()

    for which in range(3):

        @pl.when(rel == which + 1)
        def _(which=which):
            for tap, side, at, dst in plan:
                src = bufs[2 * which + side].at[pl.ds(tap * HALF, HALF)]
                pltpu.make_async_copy(src, dst, sems.at[tap, side]).start()
            pltpu.make_async_copy(bufs[2 * which].at[pl.ds(GAIN_ROW, 16)], terms, gain_sem).start()

    def wait(first, last):
        for tap, side, at, dst in plan:
            if first <= tap < last:
                pltpu.make_async_copy(
                    bufs[side].at[pl.ds(tap * HALF, HALF)], dst, sems.at[tap, side]
                ).wait()

    def gain_row(gain):
        pltpu.make_async_copy(bufs[0].at[pl.ds(GAIN_ROW, 16)], terms, gain_sem).wait()
        rows = terms[...].astype(F32)
        received = rows[0:1] + (rows[1:2] + rows[2:3])
        return jnp.where(rel == 0, gain[...], received)

    return wait, gain_row


def normed_of(values, gain_row):
    inverse = lax.rsqrt(jnp.mean(values * values, axis=-1, keepdims=True) + 1e-06)
    return (values * inverse * gain_row).astype(BF16)


def pieces(count, size):
    return [(at, min(size, count - at)) for at in range(0, count, size)]


def mix(source, weights, hidden, count, columns):
    taps = weights[0:3].reshape(3 * C, C)
    rows = columns * 16
    for at, size in pieces(count, 4):
        parts = [source[at + k : at + k + size, 0:rows].reshape(size * rows, C) for k in range(3)]
        mixed = jnp.dot(jnp.concatenate(parts, axis=-1), taps, preferred_element_type=F32)
        value = jax.nn.silu(mixed).astype(BF16).reshape(size, rows, C)
        for col in range(columns):
            hidden[col, at : at + size] = value[:, col * 16 : col * 16 + 16, :]


def spatial(hidden, weights, col, count):
    size = count * 16
    row = lax.broadcasted_iota(jnp.int32, (size, C), 0) % 16
    lhs = jnp.concatenate([hidden[col + q, 0:count].reshape(size, C) for q in range(3)], axis=-1)
    y = []
    for p in range(3):
        taps = weights[3 + 3 * p : 6 + 3 * p].reshape(3 * C, C)
        y.append(jnp.dot(lhs, taps, preferred_element_type=F32))
    down = jnp.where(row == 0, 0.0, pltpu.roll(y[0], 1, 0))
    up = jnp.where(row == 15, 0.0, pltpu.roll(y[2], size - 1, 0))
    return y[1] + down + up


def cols(col):
    return slice(col * 16, col * 16 + 16)


def pair_kernel(first, scal, gain, far, mid, left, right, *rest):
    if first:
        refs, (out, tails) = rest[:8], rest[8:10]
    else:
        refs, (out,) = rest[:8], rest[8:9]
    own, bufs = refs[:2], refs[2:]
    weights, terms, sems, gain_sem, normed, hidden, second, normed2 = rest[(10 if first else 9) :]
    section = 0 if first else 2
    total = 24 if first else 20
    mine, shard, shards = scal[0], scal[2], scal[3]
    loads = []
    for k in range(2):
        loads.append(
            fetch(section + k, scal, own, bufs, weights.at[k], terms.at[k], sems.at[k], gain_sem.at[k])
        )
    if first:
        mine_rel = lax.rem(2 - mine + SECTIONS, SECTIONS)
        for which in range(3):

            @pl.when(lax.rem(mine_rel + 2, 3) == which)
            def _(which=which):
                pltpu.make_async_copy(
                    bufs[2 * which].at[pl.ds(GAIN_ROW, 16)], terms.at[2], gain_sem.at[2]
                ).start()

    row = loads[0][1](gain)
    sources = (left, mid, right)
    for n, source in enumerate(sources):
        for at, size in pieces(total, 8):
            values = source[at : at + size].astype(F32).reshape(size * 32, C)
            normed[at : at + size, n * 32 : n * 32 + 32] = normed_of(values, row).reshape(size, 32, C)
    if first:
        tails[0] = normed[total - 2 : total, 32:64]

    @pl.when(mine == 0)
    def _():
        for n, source in enumerate(sources):
            normed[total - 18 : total - 16, n * 32 : n * 32 + 32] = source[total - 18 : total - 16]

    loads[0][0](0, 3)
    count = total - 2
    mix(normed, weights.at[0], hidden, count, 6)
    loads[0][0](3, TAPS)
    row = loads[1][1](gain)
    for col in range(4):
        source, at = ((left, cols(1)), (mid, cols(0)), (mid, cols(1)), (right, cols(0)))[col]
        a = source[2:, at, :].reshape(count * 16, C).astype(F32)
        result = (a + spatial(hidden, weights.at[0], col, count)).astype(BF16)
        if col in (1, 2):
            second[:, cols(col - 1), :] = result.reshape(count, 16, C)
        n = normed_of(result.astype(F32), row)
        if col == 0:
            n = jnp.where(shard == 0, jnp.zeros_like(n), n)
        if col == 3:
            n = jnp.where(shard == shards - 1, jnp.zeros_like(n), n)
        normed2[:, cols(col), :] = n.reshape(count, 16, C)
    own_tail = normed2[count - 2 : count, 16:48]
    if first:
        tails[1] = own_tail

    @pl.when(mine == 0)
    def _():
        for col in range(4):
            source, at = ((left, cols(1)), (mid, cols(0)), (mid, cols(1)), (right, cols(0)))[col]
            normed2[count - 18 : count - 16, cols(col)] = source[total - 20 : total - 18, at, :]

    loads[1][0](0, 3)
    count = total - 4
    mix(normed2, weights.at[1], hidden, count, 4)
    loads[1][0](3, TAPS)
    for col in range(2):
        a = second[2:, cols(col), :].reshape(count * 16, C).astype(F32)
        result = (a + spatial(hidden, weights.at[1], col, count)).astype(BF16).reshape(count, 16, C)
        if first:
            out[:, cols(col), :] = result
        else:
            for side in range(2):
                lanes = slice(side * LANES, (side + 1) * LANES)
                out[:, side * 32 + col * 16 : side * 32 + col * 16 + 16, :] = result[:, :, lanes]
    if first:
        pltpu.make_async_copy(bufs[0].at[pl.ds(GAIN_ROW, 16)], terms.at[2], gain_sem.at[2]).wait()
        rows = terms[2].astype(F32)
        received = rows[0:1] + (rows[1:2] + rows[2:3])
        row = jnp.where(mine == 2, gain[...], received)
        last = out[count - 2 : count].astype(F32).reshape(64, C)
        tails[2] = normed_of(last, row).reshape(2, 32, C)

        @pl.when(mine == 0)
        def _():
            out[0:4] = far[...]

    else:
        carry = jnp.where(mine == SECTIONS - 1, own_tail, far[...])
        for side in range(2):
            lanes = slice(side * LANES, (side + 1) * LANES)
            for n in range(4):
                out[:, 64 + 4 * side + n, :] = carry[n // 2, cols(n % 2), lanes]


def pair_call(first, scal, gain, far, sources, own, bufs):
    total = 24 if first else 20
    count = total - 2
    if first:
        outs = (shape_of(20, 32, C), shape_of(3, 2, 32, C))
    else:
        outs = shape_of(16, 72, LANES)
    return call(
        functools.partial(pair_kernel, first),
        outs,
        [SMEM] + [VMEM] * 5 + [HBM] * 8,
        [
            pltpu.VMEM((2, TAPS, C, C), BF16),
            pltpu.VMEM((3, 16, C), BF16),
            pltpu.SemaphoreType.DMA((2, TAPS, 2)),
            pltpu.SemaphoreType.DMA((3,)),
            pltpu.VMEM((total, 96, C), BF16),
            pltpu.VMEM((6, count, 16, C), BF16),
            pltpu.VMEM((count, 32, C), BF16),
            pltpu.VMEM((count, 64, C), BF16),
        ],
        flops=1 << 31,
        moved=4 << 20,
        room=58,
    )(scal, gain, far, *sources, *own, *bufs)


def join_kernel(scal, frames, before, near, carry, out):
    out[8:24] = frames[...]
    out[0:8] = before[...]

    @pl.when(scal[0] == 0)
    def _():
        out[4:6] = near[...]
        out[6:8] = carry[...]


def body(latents, norm_gain, time_weight, space_weight, carry_in):
    shards = lax.axis_size("shard")
    streams = lax.axis_size("stream")
    mine = lax.axis_index("segment")
    core = lax.rem(lax.axis_index("stream"), 2)
    here = lax.axis_index("shard")
    scal = jnp.stack([mine, core, here, jnp.int32(shards)]).astype(jnp.int32)

    def ring(distance):
        return [(i, (i + distance) % SECTIONS) for i in range(SECTIONS)]

    def over_segments(array, pairs):
        return lax.ppermute(array, "segment", pairs)

    swap = [(i, i ^ 1) for i in range(streams)]
    up = [(i, i + 1) for i in range(shards - 1)]
    down = [(i + 1, i) for i in range(shards - 1)]

    block = lax.dynamic_index_in_dim(latents, mine, 0, keepdims=False)[0]
    chunks = call(chunk_kernel, shape_of(16, 72, LANES), [VMEM] * 2)(
        block.transpose(1, 0, 2), carry_in[0, :, 0]
    )
    got = lax.all_to_all(chunks, "shard", split_axis=0, concat_axis=0, tiled=True)

    packed = call(
        pack_kernel,
        shape_of(PACKED, C),
        [SMEM, VMEM, HBM, HBM],
        [pltpu.SemaphoreType.DMA((TAPS,))],
        room=58,
    )(scal, norm_gain, time_weight, space_weight)
    bufs = []
    for distance in (-1, 2, 1):
        buf = over_segments(packed, ring(distance))
        bufs += [buf, lax.ppermute(buf, "stream", swap)]

    frames, sent_before, carry = call(
        unpack_kernel, (shape_of(16, 32, C), shape_of(8, 32, C), shape_of(2, 32, C)), [VMEM]
    )(got)
    before = over_segments(sent_before, [(0, 1), (1, 2), (2, 3)])
    near = over_segments(carry, [(1, 0), (3, 2)])
    far = over_segments(jnp.concatenate([near, carry], axis=0), [(2, 0)])
    joined = call(join_kernel, shape_of(24, 32, C), [SMEM] + [VMEM] * 4)(
        scal, frames, before, near, carry
    )

    def beside(array):
        came_left = lax.ppermute(array, "shard", up)
        came_right = lax.ppermute(array, "shard", down)
        return array, came_left, came_right

    own = (time_weight, space_weight)
    middle, tails = pair_call(True, scal, norm_gain, far, beside(joined), own, bufs)
    sources = beside(middle)
    over = over_segments(tails[1:3].reshape(4, 32, C), [(3, 2)])
    wrapped = over_segments(jnp.where(mine == 3, tails[0], over[0:2]), [(3, 0), (2, 1)])
    carry = jnp.where(mine == 2, over[2:4], wrapped)
    out = pair_call(False, scal, norm_gain, carry, sources, own, bufs)
    sent = lax.all_to_all(out, "shard", split_axis=0, concat_axis=0, tiled=True)
    main = jnp.concatenate([sent[:, 0:32], sent[:, 32:64]], axis=-1)
    decoded = main.reshape(32, 16, C).transpose(1, 0, 2)[None, None]
    kept_rows = jnp.concatenate([sent[:, 64:68], sent[:, 68:72]], axis=-1)
    carry_out = kept_rows.reshape(shards, 2, 2, C).transpose(1, 0, 2, 3).reshape(1, 2, 1, 32, C)
    return (decoded, carry_out)


def solution(mesh):
    placed = (
        P("stream", "shard", None, None, None),
        P("segment", None),
        P("segment", None, None, None),
        P("segment", None, None, None),
        P("segment", "stream", "shard", None, None),
    )
    return jax.shard_map(
        body,
        mesh=mesh,
        in_specs=placed,
        out_specs=(
            P(("stream", "segment"), "shard", None, None, None),
            P("segment", "stream", "shard", None, None),
        ),
        check_vma=False,
    )
```

```python
import functools

import jax
import jax.numpy as jnp
from jax import lax
from jax.experimental import pallas as pl
from jax.experimental.pallas import tpu as pltpu
from jax.sharding import PartitionSpec as P


C = 256
LANES = 128
HALF = 128
TAPS = 12
GAIN_ROW = TAPS * HALF
PACKED = GAIN_ROW + 16
SECTIONS = 4
F32 = jnp.float32
BF16 = jnp.bfloat16

VMEM = pl.BlockSpec(memory_space=pltpu.VMEM)
HBM = pl.BlockSpec(memory_space=pltpu.HBM)


def core_of():
    return lax.rem(lax.axis_index("stream"), 2)


def shape_of(*dims, dtype=BF16):
    return jax.ShapeDtypeStruct(dims, dtype)


def call(kernel, outs, in_specs, scratch=(), flops=1 << 20, moved=1 << 20, room=16):
    out_specs = tuple(VMEM for _ in outs) if isinstance(outs, tuple) else VMEM
    return pl.pallas_call(
        kernel,
        out_shape=outs,
        in_specs=in_specs,
        out_specs=out_specs,
        scratch_shapes=list(scratch),
        cost_estimate=pl.CostEstimate(flops=flops, bytes_accessed=moved, transcendentals=0),
        compiler_params=pltpu.CompilerParams(vmem_limit_bytes=room << 20),
    )


def chunk_kernel(columns, row, out):
    flat = columns[...].reshape(16, 32, C)
    for side in range(2):
        lanes = slice(side * LANES, (side + 1) * LANES)
        out[:, side * 32 : side * 32 + 32, :] = flat[:, :, lanes]
        for frame in range(2):
            at = 64 + 4 * side + 2 * frame
            for z in range(16):
                out[z, at : at + 2, :] = row[frame, 2 * z : 2 * z + 2, lanes]


def pack_kernel(gain, taps_time, taps_space, out, sems):
    at = pl.multiple_of(core_of() * HALF, HALF)
    copies = []
    for tap in range(TAPS):
        own = taps_time.at[0, tap] if tap < 3 else taps_space.at[0, tap - 3]
        copies.append(
            pltpu.make_async_copy(own.at[pl.ds(at, HALF)], out.at[pl.ds(tap * HALF, HALF)], sems.at[tap])
        )
        copies[-1].start()
    value = gain[...]
    high = value.astype(BF16)
    rest = value - high.astype(F32)
    middle = rest.astype(BF16)
    low = (rest - middle.astype(F32)).astype(BF16)
    pick = lax.broadcasted_iota(jnp.int32, (16, C), 0)
    rows = jnp.where(pick == 0, high.astype(F32), 0.0)
    rows = jnp.where(pick == 1, middle.astype(F32), rows)
    rows = jnp.where(pick == 2, low.astype(F32), rows)
    for copy in copies:
        copy.wait()
    out[GAIN_ROW:PACKED, :] = rows.astype(BF16)


def unpack_kernel(got, frames, before, carry):
    for side in range(2):
        lanes = slice(side * LANES, (side + 1) * LANES)
        block = got[:, side * 32 : side * 32 + 32, :]
        frames[:, :, lanes] = block
        before[:, :, lanes] = block[8:16]
        for n in range(4):
            frame, col = n // 2, n % 2
            carry[frame, col * 16 : col * 16 + 16, lanes] = got[:, 64 + 4 * side + n, :]


def fetch(section, own, bufs, out, terms, sems, gain_sem):
    mine, core = lax.axis_index("segment"), core_of()
    rel = lax.rem(section - mine + SECTIONS, SECTIONS)
    plan = []
    for tap in range(TAPS):
        for side in range(2):
            at = pl.multiple_of((core if side == 0 else 1 - core) * HALF, HALF)
            plan.append((tap, side, at, out.at[tap, pl.ds(at, HALF)]))
    taps_time, taps_space = own

    @pl.when(rel == 0)
    def _():
        for tap, side, at, dst in plan:
            src = taps_time.at[0, tap] if tap < 3 else taps_space.at[0, tap - 3]
            pltpu.make_async_copy(src.at[pl.ds(at, HALF)], dst, sems.at[tap, side]).start()
        pltpu.make_async_copy(bufs[0].at[pl.ds(GAIN_ROW, 16)], terms, gain_sem).start()

    for which in range(3):

        @pl.when(rel == which + 1)
        def _(which=which):
            for tap, side, at, dst in plan:
                src = bufs[2 * which + side].at[pl.ds(tap * HALF, HALF)]
                pltpu.make_async_copy(src, dst, sems.at[tap, side]).start()
            pltpu.make_async_copy(bufs[2 * which].at[pl.ds(GAIN_ROW, 16)], terms, gain_sem).start()

    def wait(first, last):
        for tap, side, at, dst in plan:
            if first <= tap < last:
                pltpu.make_async_copy(
                    bufs[side].at[pl.ds(tap * HALF, HALF)], dst, sems.at[tap, side]
                ).wait()

    def gain_row(gain):
        pltpu.make_async_copy(bufs[0].at[pl.ds(GAIN_ROW, 16)], terms, gain_sem).wait()
        rows = terms[...].astype(F32)
        received = rows[0:1] + (rows[1:2] + rows[2:3])
        return jnp.where(rel == 0, gain[...], received)

    return wait, gain_row


def normed_of(values, gain_row):
    inverse = lax.rsqrt(jnp.mean(values * values, axis=-1, keepdims=True) + 1e-06)
    return (values * inverse * gain_row).astype(BF16)


def pieces(count, size):
    return [(at, min(size, count - at)) for at in range(0, count, size)]


def mix(source, weights, hidden, count, columns):
    taps = weights[0:3].reshape(3 * C, C)
    rows = columns * 16
    for at, size in pieces(count, 4):
        parts = [source[at + k : at + k + size, 0:rows].reshape(size * rows, C) for k in range(3)]
        mixed = jnp.dot(jnp.concatenate(parts, axis=-1), taps, preferred_element_type=F32)
        value = jax.nn.silu(mixed).astype(BF16).reshape(size, rows, C)
        for col in range(columns):
            hidden[col, at : at + size] = value[:, col * 16 : col * 16 + 16, :]


def spatial(hidden, weights, col, count):
    size = count * 16
    row = lax.broadcasted_iota(jnp.int32, (size, C), 0) % 16
    lhs = jnp.concatenate([hidden[col + q, 0:count].reshape(size, C) for q in range(3)], axis=-1)
    y = []
    for p in range(3):
        taps = weights[3 + 3 * p : 6 + 3 * p].reshape(3 * C, C)
        y.append(jnp.dot(lhs, taps, preferred_element_type=F32))
    down = jnp.where(row == 0, 0.0, pltpu.roll(y[0], 1, 0))
    up = jnp.where(row == 15, 0.0, pltpu.roll(y[2], size - 1, 0))
    return y[1] + down + up


def cols(col):
    return slice(col * 16, col * 16 + 16)


def pair_kernel(first, gain, far, wrapped, mid, left, right, *rest):
    if first:
        refs, (out, tails, tails_near) = rest[:8], rest[8:11]
    else:
        refs, (out,) = rest[:8], rest[8:9]
    own, bufs = refs[:2], refs[2:]
    weights, terms, sems, gain_sem, normed, hidden, second, normed2 = rest[(11 if first else 9) :]
    section = 0 if first else 2
    total = 24 if first else 20
    mine, shard = lax.axis_index("segment"), lax.axis_index("shard")
    shards = lax.axis_size("shard")
    loads = []
    for k in range(2):
        loads.append(
            fetch(section + k, own, bufs, weights.at[k], terms.at[k], sems.at[k], gain_sem.at[k])
        )
    if first:
        mine_rel = lax.rem(2 - mine + SECTIONS, SECTIONS)
        for which in range(3):

            @pl.when(lax.rem(mine_rel + 2, 3) == which)
            def _(which=which):
                pltpu.make_async_copy(
                    bufs[2 * which].at[pl.ds(GAIN_ROW, 16)], terms.at[2], gain_sem.at[2]
                ).start()

    row = loads[0][1](gain)
    sources = (left, mid, right)
    for n, source in enumerate(sources):
        for at, size in pieces(total, 8):
            values = source[at : at + size].astype(F32).reshape(size * 32, C)
            normed[at : at + size, n * 32 : n * 32 + 32] = normed_of(values, row).reshape(size, 32, C)
    if first:
        tails[...] = normed[total - 2 : total, 32:64]

    @pl.when(mine == 0)
    def _():
        for n, source in enumerate(sources):
            normed[total - 18 : total - 16, n * 32 : n * 32 + 32] = source[total - 18 : total - 16]

    loads[0][0](0, 3)
    count = total - 2
    mix(normed, weights.at[0], hidden, count, 6)
    loads[0][0](3, TAPS)
    row = loads[1][1](gain)
    for col in range(4):
        source, at = ((left, cols(1)), (mid, cols(0)), (mid, cols(1)), (right, cols(0)))[col]
        a = source[2:, at, :].reshape(count * 16, C).astype(F32)
        result = (a + spatial(hidden, weights.at[0], col, count)).astype(BF16)
        if col in (1, 2):
            second[:, cols(col - 1), :] = result.reshape(count, 16, C)
        n = normed_of(result.astype(F32), row)
        if col == 0:
            n = jnp.where(shard == 0, jnp.zeros_like(n), n)
        if col == 3:
            n = jnp.where(shard == shards - 1, jnp.zeros_like(n), n)
        normed2[:, cols(col), :] = n.reshape(count, 16, C)
    own_tail = normed2[count - 2 : count, 16:48]
    if first:
        tails_near[0:2] = own_tail

    @pl.when(mine == 0)
    def _():
        for col in range(4):
            source, at = ((left, cols(1)), (mid, cols(0)), (mid, cols(1)), (right, cols(0)))[col]
            normed2[count - 18 : count - 16, cols(col)] = source[total - 20 : total - 18, at, :]

    loads[1][0](0, 3)
    count = total - 4
    mix(normed2, weights.at[1], hidden, count, 4)
    loads[1][0](3, TAPS)
    for col in range(2):
        a = second[2:, cols(col), :].reshape(count * 16, C).astype(F32)
        result = (a + spatial(hidden, weights.at[1], col, count)).astype(BF16).reshape(count, 16, C)
        if first:
            out[:, cols(col), :] = result
        else:
            for side in range(2):
                lanes = slice(side * LANES, (side + 1) * LANES)
                out[:, side * 32 + col * 16 : side * 32 + col * 16 + 16, :] = result[:, :, lanes]
    if first:
        pltpu.make_async_copy(bufs[0].at[pl.ds(GAIN_ROW, 16)], terms.at[2], gain_sem.at[2]).wait()
        rows = terms[2].astype(F32)
        received = rows[0:1] + (rows[1:2] + rows[2:3])
        row = jnp.where(mine == 2, gain[...], received)
        last = out[count - 2 : count].astype(F32).reshape(64, C)
        tails_near[2:4] = normed_of(last, row).reshape(2, 32, C)

        @pl.when(mine == 0)
        def _():
            out[0:4] = far[...]

    else:
        carry = jnp.where(mine == 2, far[2:4], wrapped[...])
        carry = jnp.where(mine == SECTIONS - 1, own_tail, carry)
        for side in range(2):
            lanes = slice(side * LANES, (side + 1) * LANES)
            for n in range(4):
                out[:, 64 + 4 * side + n, :] = carry[n // 2, cols(n % 2), lanes]


def pair_call(first, gain, far, wrapped, sources, own, bufs):
    total = 24 if first else 20
    count = total - 2
    if first:
        outs = (shape_of(20, 32, C), shape_of(2, 32, C), shape_of(4, 32, C))
    else:
        outs = shape_of(16, 72, LANES)
    return call(
        functools.partial(pair_kernel, first),
        outs,
        [VMEM] * 6 + [HBM] * 8,
        [
            pltpu.VMEM((2, TAPS, C, C), BF16),
            pltpu.VMEM((3, 16, C), BF16),
            pltpu.SemaphoreType.DMA((2, TAPS, 2)),
            pltpu.SemaphoreType.DMA((3,)),
            pltpu.VMEM((total, 96, C), BF16),
            pltpu.VMEM((6, count, 16, C), BF16),
            pltpu.VMEM((count, 32, C), BF16),
            pltpu.VMEM((count, 64, C), BF16),
        ],
        flops=1 << 31,
        moved=4 << 20,
    )(gain, far, wrapped, *sources, *own, *bufs)


def join_kernel(frames, before, near, carry, out, both):
    out[8:24] = frames[...]
    out[0:8] = before[...]
    both[0:2] = near[...]
    both[2:4] = carry[...]

    @pl.when(lax.axis_index("segment") == 0)
    def _():
        out[4:6] = near[...]
        out[6:8] = carry[...]


def choose_kernel(own, came, out):
    out[...] = jnp.where(lax.axis_index("segment") == SECTIONS - 1, own[...], came[0:2])


def body(latents, norm_gain, time_weight, space_weight, carry_in):
    shards = lax.axis_size("shard")
    streams = lax.axis_size("stream")
    mine = lax.axis_index("segment")

    def ring(distance):
        return [(i, (i + distance) % SECTIONS) for i in range(SECTIONS)]

    def over_segments(array, pairs):
        return lax.ppermute(array, "segment", pairs)

    swap = [(i, i ^ 1) for i in range(streams)]
    up = [(i, i + 1) for i in range(shards - 1)]
    down = [(i + 1, i) for i in range(shards - 1)]

    block = lax.dynamic_index_in_dim(latents, mine, 0, keepdims=False)[0]
    chunks = call(chunk_kernel, shape_of(16, 72, LANES), [VMEM] * 2)(
        block.transpose(1, 0, 2), carry_in[0, :, 0]
    )
    got = lax.all_to_all(chunks, "shard", split_axis=0, concat_axis=0, tiled=True)

    packed = call(
        pack_kernel,
        shape_of(PACKED, C),
        [VMEM, HBM, HBM],
        [pltpu.SemaphoreType.DMA((TAPS,))],
        room=58,
    )(norm_gain, time_weight, space_weight)
    bufs = []
    for distance in (-1, 2, 1):
        buf = over_segments(packed, ring(distance))
        bufs += [buf, lax.ppermute(buf, "stream", swap)]

    frames, sent_before, carry = call(
        unpack_kernel, (shape_of(16, 32, C), shape_of(8, 32, C), shape_of(2, 32, C)), [VMEM]
    )(got)
    before = over_segments(sent_before, [(0, 1), (1, 2), (2, 3)])
    near = over_segments(carry, [(1, 0), (3, 2)])
    joined, both = call(join_kernel, (shape_of(24, 32, C), shape_of(4, 32, C)), [VMEM] * 4)(
        frames, before, near, carry
    )
    far = over_segments(both, [(2, 0)])

    def beside(array):
        came_left = lax.ppermute(array, "shard", up)
        came_right = lax.ppermute(array, "shard", down)
        return array, came_left, came_right

    own = (time_weight, space_weight)
    middle, tail, tails_near = pair_call(True, norm_gain, far, carry, beside(joined), own, bufs)
    sources = beside(middle)
    over = over_segments(tails_near, [(3, 2)])
    chosen = call(choose_kernel, shape_of(2, 32, C), [VMEM] * 2)(tail, over)
    wrapped = over_segments(chosen, [(3, 0), (2, 1)])
    out = pair_call(False, norm_gain, over, wrapped, sources, own, bufs)
    sent = lax.all_to_all(out, "shard", split_axis=0, concat_axis=0, tiled=True)
    main = jnp.concatenate([sent[:, 0:32], sent[:, 32:64]], axis=-1)
    decoded = main.reshape(32, 16, C).transpose(1, 0, 2)[None, None]
    kept_rows = jnp.concatenate([sent[:, 64:68], sent[:, 68:72]], axis=-1)
    carry_out = kept_rows.reshape(shards, 2, 2, C).transpose(1, 0, 2, 3).reshape(1, 2, 1, 32, C)
    return (decoded, carry_out)


def solution(mesh):
    placed = (
        P("stream", "shard", None, None, None),
        P("segment", None),
        P("segment", None, None, None),
        P("segment", None, None, None),
        P("segment", "stream", "shard", None, None),
    )
    return jax.shard_map(
        body,
        mesh=mesh,
        in_specs=placed,
        out_specs=(
            P(("stream", "segment"), "shard", None, None, None),
            P("segment", "stream", "shard", None, None),
        ),
        check_vma=False,
    )
```

```python
import functools

import jax
import jax.numpy as jnp
from jax import lax
from jax.experimental import pallas as pl
from jax.experimental.pallas import tpu as pltpu
from jax.sharding import PartitionSpec as P


C = 256
LANES = 128
HALF = 128
TAPS = 12
GAIN_ROW = TAPS * HALF
PACKED = GAIN_ROW + 16
SECTIONS = 4
F32 = jnp.float32
BF16 = jnp.bfloat16

VMEM = pl.BlockSpec(memory_space=pltpu.VMEM)
HBM = pl.BlockSpec(memory_space=pltpu.HBM)


def core_of():
    return lax.rem(lax.axis_index("stream"), 2)


def shape_of(*dims, dtype=BF16):
    return jax.ShapeDtypeStruct(dims, dtype)


def call(kernel, outs, in_specs, scratch=(), flops=1 << 20, moved=1 << 20, room=16):
    out_specs = tuple(VMEM for _ in outs) if isinstance(outs, tuple) else VMEM
    return pl.pallas_call(
        kernel,
        out_shape=outs,
        in_specs=in_specs,
        out_specs=out_specs,
        scratch_shapes=list(scratch),
        cost_estimate=pl.CostEstimate(flops=flops, bytes_accessed=moved, transcendentals=0),
        compiler_params=pltpu.CompilerParams(vmem_limit_bytes=room << 20),
    )


def chunk_kernel(columns, row, out):
    flat = columns[...].reshape(16, 32, C)
    for side in range(2):
        lanes = slice(side * LANES, (side + 1) * LANES)
        out[:, side * 32 : side * 32 + 32, :] = flat[:, :, lanes]
        for frame in range(2):
            at = 64 + 4 * side + 2 * frame
            for z in range(16):
                out[z, at : at + 2, :] = row[frame, 2 * z : 2 * z + 2, lanes]


def pack_kernel(gain, taps_time, taps_space, out, sems):
    at = pl.multiple_of(core_of() * HALF, HALF)
    copies = []
    for tap in range(TAPS):
        own = taps_time.at[0, tap] if tap < 3 else taps_space.at[0, tap - 3]
        copies.append(
            pltpu.make_async_copy(own.at[pl.ds(at, HALF)], out.at[pl.ds(tap * HALF, HALF)], sems.at[tap])
        )
        copies[-1].start()
    value = gain[...]
    high = value.astype(BF16)
    rest = value - high.astype(F32)
    middle = rest.astype(BF16)
    low = (rest - middle.astype(F32)).astype(BF16)
    pick = lax.broadcasted_iota(jnp.int32, (16, C), 0)
    rows = jnp.where(pick == 0, high.astype(F32), 0.0)
    rows = jnp.where(pick == 1, middle.astype(F32), rows)
    rows = jnp.where(pick == 2, low.astype(F32), rows)
    for copy in copies:
        copy.wait()
    out[GAIN_ROW:PACKED, :] = rows.astype(BF16)


def unpack_kernel(got, frames, before, carry):
    for side in range(2):
        lanes = slice(side * LANES, (side + 1) * LANES)
        block = got[:, side * 32 : side * 32 + 32, :]
        frames[:, :, lanes] = block
        before[:, :, lanes] = block[8:16]
        for n in range(4):
            frame, col = n // 2, n % 2
            carry[frame, col * 16 : col * 16 + 16, lanes] = got[:, 64 + 4 * side + n, :]


def stack_kernel(*refs):
    bufs, out, sems = refs[:SECTIONS], refs[SECTIONS], refs[SECTIONS + 1]
    copies = []
    for which, buf in enumerate(bufs):
        to = out.at[pl.ds(which * PACKED, PACKED)]
        copies.append(pltpu.make_async_copy(buf, to, sems.at[which]))
        copies[-1].start()
    for copy in copies:
        copy.wait()


GROUPS = ((0, 3), (3, TAPS))


def base_of(section):
    rel = lax.rem(section - lax.axis_index("segment") + SECTIONS, SECTIONS)
    return pl.multiple_of(rel * PACKED, 16)


def fetch(section, bufs, out, terms, sems, gain_sem):
    core = core_of()
    base = base_of(section)
    gain_copy = pltpu.make_async_copy(bufs[0].at[pl.ds(base + GAIN_ROW, 16)], terms, gain_sem)
    gain_copy.start()
    copies = []
    for first, last in GROUPS:
        at, size = first * HALF, (last - first) * HALF
        for part in range(2):
            side = core if part == 0 else 1 - core
            src = bufs[part].at[pl.ds(pl.multiple_of(base + at, 16), size)]
            copies.append(
                pltpu.make_async_copy(src, out.at[side, pl.ds(at, size)], sems.at[len(copies)])
            )
            copies[-1].start()

    def wait(group):
        copies[2 * group].wait()
        copies[2 * group + 1].wait()

    def gain_row():
        gain_copy.wait()
        rows = terms[...].astype(F32)
        return rows[0:1] + (rows[1:2] + rows[2:3])

    return wait, gain_row


def times_taps(parts, weights, tap):
    rows = slice(tap * HALF, (tap + 3) * HALF)
    lhs = [part[:, side * HALF : (side + 1) * HALF] for side in range(2) for part in parts]
    taps = jnp.concatenate([weights[0, rows], weights[1, rows]], axis=0)
    return jnp.dot(jnp.concatenate(lhs, axis=-1), taps, preferred_element_type=F32)


def normed_of(values, gain_row):
    inverse = lax.rsqrt(jnp.mean(values * values, axis=-1, keepdims=True) + 1e-06)
    return (values * inverse * gain_row).astype(BF16)


def pieces(count, size):
    return [(at, min(size, count - at)) for at in range(0, count, size)]


def mix(source, weights, hidden, count, columns):
    rows = columns * 16
    for at, size in pieces(count, 4):
        parts = [source[at + k : at + k + size, 0:rows].reshape(size * rows, C) for k in range(3)]
        mixed = times_taps(parts, weights, 0)
        value = jax.nn.silu(mixed).astype(BF16).reshape(size, rows, C)
        for col in range(columns):
            hidden[col, at : at + size] = value[:, col * 16 : col * 16 + 16, :]


def spatial(hidden, weights, col, count):
    size = count * 16
    row = lax.broadcasted_iota(jnp.int32, (size, C), 0) % 16
    parts = [hidden[col + q, 0:count].reshape(size, C) for q in range(3)]
    y = [times_taps(parts, weights, 3 + 3 * p) for p in range(3)]
    down = jnp.where(row == 0, 0.0, pltpu.roll(y[0], 1, 0))
    up = jnp.where(row == 15, 0.0, pltpu.roll(y[2], size - 1, 0))
    return y[1] + down + up


def cols(col):
    return slice(col * 16, col * 16 + 16)


def pair_kernel(first, far, wrapped, mid, left, right, stacked, swapped, *rest):
    if first:
        out, tails, tails_near = rest[:3]
    else:
        (out,) = rest[:1]
    weights, terms, sems, gain_sem, normed, hidden, second, normed2 = rest[-8:]
    bufs = (stacked, swapped)
    section = 0 if first else 2
    total = 24 if first else 20
    mine, shard = lax.axis_index("segment"), lax.axis_index("shard")
    shards = lax.axis_size("shard")
    loads = []
    for k in range(2):
        loads.append(
            fetch(section + k, bufs, weights.at[k], terms.at[k], sems.at[k], gain_sem.at[k])
        )
    last_gain = pltpu.make_async_copy(
        stacked.at[pl.ds(base_of(2) + GAIN_ROW, 16)], terms.at[2], gain_sem.at[2]
    )
    if first:
        last_gain.start()
    row = loads[0][1]()
    sources = (left, mid, right)
    for n, source in enumerate(sources):
        for at, size in pieces(total, 8):
            values = source[at : at + size].astype(F32).reshape(size * 32, C)
            normed[at : at + size, n * 32 : n * 32 + 32] = normed_of(values, row).reshape(size, 32, C)
    if first:
        tails[...] = normed[total - 2 : total, 32:64]

    @pl.when(mine == 0)
    def _():
        for n, source in enumerate(sources):
            normed[total - 18 : total - 16, n * 32 : n * 32 + 32] = source[total - 18 : total - 16]

    loads[0][0](0)
    count = total - 2
    mix(normed, weights.at[0], hidden, count, 6)
    loads[0][0](1)
    row = loads[1][1]()
    for col in range(4):
        source, at = ((left, cols(1)), (mid, cols(0)), (mid, cols(1)), (right, cols(0)))[col]
        a = source[2:, at, :].reshape(count * 16, C).astype(F32)
        result = (a + spatial(hidden, weights.at[0], col, count)).astype(BF16)
        if col in (1, 2):
            second[:, cols(col - 1), :] = result.reshape(count, 16, C)
        n = normed_of(result.astype(F32), row)
        if col == 0:
            n = jnp.where(shard == 0, jnp.zeros_like(n), n)
        if col == 3:
            n = jnp.where(shard == shards - 1, jnp.zeros_like(n), n)
        normed2[:, cols(col), :] = n.reshape(count, 16, C)
    own_tail = normed2[count - 2 : count, 16:48]
    if first:
        tails_near[0:2] = own_tail

    @pl.when(mine == 0)
    def _():
        for col in range(4):
            source, at = ((left, cols(1)), (mid, cols(0)), (mid, cols(1)), (right, cols(0)))[col]
            normed2[count - 18 : count - 16, cols(col)] = source[total - 20 : total - 18, at, :]

    loads[1][0](0)
    count = total - 4
    mix(normed2, weights.at[1], hidden, count, 4)
    loads[1][0](1)
    for col in range(2):
        a = second[2:, cols(col), :].reshape(count * 16, C).astype(F32)
        result = (a + spatial(hidden, weights.at[1], col, count)).astype(BF16).reshape(count, 16, C)
        if first:
            out[:, cols(col), :] = result
        else:
            for side in range(2):
                lanes = slice(side * LANES, (side + 1) * LANES)
                out[:, side * 32 + col * 16 : side * 32 + col * 16 + 16, :] = result[:, :, lanes]
    if first:
        last_gain.wait()
        rows = terms[2].astype(F32)
        row = rows[0:1] + (rows[1:2] + rows[2:3])
        last = out[count - 2 : count].astype(F32).reshape(64, C)
        tails_near[2:4] = normed_of(last, row).reshape(2, 32, C)

        @pl.when(mine == 0)
        def _():
            out[0:4] = far[...]

    else:
        carry = jnp.where(mine == 2, far[2:4], wrapped[...])
        carry = jnp.where(mine == SECTIONS - 1, own_tail, carry)
        for side in range(2):
            lanes = slice(side * LANES, (side + 1) * LANES)
            for n in range(4):
                out[:, 64 + 4 * side + n, :] = carry[n // 2, cols(n % 2), lanes]


def pair_call(first, far, wrapped, sources, bufs):
    total = 24 if first else 20
    count = total - 2
    if first:
        outs = (shape_of(20, 32, C), shape_of(2, 32, C), shape_of(4, 32, C))
    else:
        outs = shape_of(16, 72, LANES)
    return call(
        functools.partial(pair_kernel, first),
        outs,
        [VMEM] * 5 + [HBM] * 2,
        [
            pltpu.VMEM((2, 2, GAIN_ROW, C), BF16),
            pltpu.VMEM((3, 16, C), BF16),
            pltpu.SemaphoreType.DMA((2, 4)),
            pltpu.SemaphoreType.DMA((3,)),
            pltpu.VMEM((total, 96, C), BF16),
            pltpu.VMEM((6, count, 16, C), BF16),
            pltpu.VMEM((count, 32, C), BF16),
            pltpu.VMEM((count, 64, C), BF16),
        ],
        flops=1 << 31,
        moved=4 << 20,
    )(far, wrapped, *sources, *bufs)


def join_kernel(frames, before, near, carry, out, both):
    out[8:24] = frames[...]
    out[0:8] = before[...]
    both[0:2] = near[...]
    both[2:4] = carry[...]

    @pl.when(lax.axis_index("segment") == 0)
    def _():
        out[4:6] = near[...]
        out[6:8] = carry[...]


def choose_kernel(own, came, out):
    out[...] = jnp.where(lax.axis_index("segment") == SECTIONS - 1, own[...], came[0:2])


def body(latents, norm_gain, time_weight, space_weight, carry_in):
    shards = lax.axis_size("shard")
    streams = lax.axis_size("stream")
    mine = lax.axis_index("segment")

    def ring(distance):
        return [(i, (i + distance) % SECTIONS) for i in range(SECTIONS)]

    def over_segments(array, pairs):
        return lax.ppermute(array, "segment", pairs)

    swap = [(i, i ^ 1) for i in range(streams)]
    up = [(i, i + 1) for i in range(shards - 1)]
    down = [(i + 1, i) for i in range(shards - 1)]

    block = lax.dynamic_index_in_dim(latents, mine, 0, keepdims=False)[0]
    chunks = call(chunk_kernel, shape_of(16, 72, LANES), [VMEM] * 2)(
        block.transpose(1, 0, 2), carry_in[0, :, 0]
    )
    got = lax.all_to_all(chunks, "shard", split_axis=0, concat_axis=0, tiled=True)

    packed = call(
        pack_kernel,
        shape_of(PACKED, C),
        [VMEM, HBM, HBM],
        [pltpu.SemaphoreType.DMA((TAPS,))],
        room=58,
    )(norm_gain, time_weight, space_weight)
    halves = [packed]
    for distance in (-1, 2, 1):
        halves.append(over_segments(packed, ring(distance)))
    stacked = call(
        stack_kernel,
        shape_of(SECTIONS * PACKED, C),
        [HBM] * SECTIONS,
        [pltpu.SemaphoreType.DMA((SECTIONS,))],
    )(*halves)
    bufs = (stacked, lax.ppermute(stacked, "stream", swap))

    frames, sent_before, carry = call(
        unpack_kernel, (shape_of(16, 32, C), shape_of(8, 32, C), shape_of(2, 32, C)), [VMEM]
    )(got)
    before = over_segments(sent_before, [(0, 1), (1, 2), (2, 3)])
    near = over_segments(carry, [(1, 0), (3, 2)])
    joined, both = call(join_kernel, (shape_of(24, 32, C), shape_of(4, 32, C)), [VMEM] * 4)(
        frames, before, near, carry
    )
    far = over_segments(both, [(2, 0)])

    def beside(array):
        came_left = lax.ppermute(array, "shard", up)
        came_right = lax.ppermute(array, "shard", down)
        return array, came_left, came_right

    middle, tail, tails_near = pair_call(True, far, carry, beside(joined), bufs)
    sources = beside(middle)
    over = over_segments(tails_near, [(3, 2)])
    chosen = call(choose_kernel, shape_of(2, 32, C), [VMEM] * 2)(tail, over)
    wrapped = over_segments(chosen, [(3, 0), (2, 1)])
    out = pair_call(False, over, wrapped, sources, bufs)
    sent = lax.all_to_all(out, "shard", split_axis=0, concat_axis=0, tiled=True)
    main = jnp.concatenate([sent[:, 0:32], sent[:, 32:64]], axis=-1)
    decoded = main.reshape(32, 16, C).transpose(1, 0, 2)[None, None]
    kept_rows = jnp.concatenate([sent[:, 64:68], sent[:, 68:72]], axis=-1)
    carry_out = kept_rows.reshape(shards, 2, 2, C).transpose(1, 0, 2, 3).reshape(1, 2, 1, 32, C)
    return (decoded, carry_out)


def solution(mesh):
    placed = (
        P("stream", "shard", None, None, None),
        P("segment", None),
        P("segment", None, None, None),
        P("segment", None, None, None),
        P("segment", "stream", "shard", None, None),
    )
    return jax.shard_map(
        body,
        mesh=mesh,
        in_specs=placed,
        out_specs=(
            P(("stream", "segment"), "shard", None, None, None),
            P("segment", "stream", "shard", None, None),
        ),
        check_vma=False,
    )
```

```python
import functools

import jax
import jax.numpy as jnp
from jax import lax
from jax.experimental import pallas as pl
from jax.experimental.pallas import tpu as pltpu
from jax.sharding import PartitionSpec as P


C = 256
LANES = 128
HALF = 128
TAPS = 12
GAIN_ROW = TAPS * HALF
PACKED = GAIN_ROW + 16
SECTIONS = 4
F32 = jnp.float32
BF16 = jnp.bfloat16

VMEM = pl.BlockSpec(memory_space=pltpu.VMEM)
HBM = pl.BlockSpec(memory_space=pltpu.HBM)


def core_of():
    return lax.rem(lax.axis_index("stream"), 2)


def shape_of(*dims, dtype=BF16):
    return jax.ShapeDtypeStruct(dims, dtype)


def call(kernel, outs, in_specs, scratch=(), flops=1 << 20, moved=1 << 20, room=16):
    out_specs = tuple(VMEM for _ in outs) if isinstance(outs, tuple) else VMEM
    return pl.pallas_call(
        kernel,
        out_shape=outs,
        in_specs=in_specs,
        out_specs=out_specs,
        scratch_shapes=list(scratch),
        cost_estimate=pl.CostEstimate(flops=flops, bytes_accessed=moved, transcendentals=0),
        compiler_params=pltpu.CompilerParams(vmem_limit_bytes=room << 20),
    )


def chunk_kernel(columns, row, out):
    flat = columns[...].reshape(16, 32, C)
    for side in range(2):
        lanes = slice(side * LANES, (side + 1) * LANES)
        out[:, side * 32 : side * 32 + 32, :] = flat[:, :, lanes]
        for frame in range(2):
            at = 64 + 4 * side + 2 * frame
            for z in range(16):
                out[z, at : at + 2, :] = row[frame, 2 * z : 2 * z + 2, lanes]


def pack_kernel(gain, taps_time, taps_space, out, sems):
    at = pl.multiple_of(core_of() * HALF, HALF)
    copies = []
    for tap in range(TAPS):
        own = taps_time.at[0, tap] if tap < 3 else taps_space.at[0, tap - 3]
        copies.append(
            pltpu.make_async_copy(own.at[pl.ds(at, HALF)], out.at[pl.ds(tap * HALF, HALF)], sems.at[tap])
        )
        copies[-1].start()
    value = gain[...]
    high = value.astype(BF16)
    rest = value - high.astype(F32)
    middle = rest.astype(BF16)
    low = (rest - middle.astype(F32)).astype(BF16)
    pick = lax.broadcasted_iota(jnp.int32, (16, C), 0)
    rows = jnp.where(pick == 0, high.astype(F32), 0.0)
    rows = jnp.where(pick == 1, middle.astype(F32), rows)
    rows = jnp.where(pick == 2, low.astype(F32), rows)
    for copy in copies:
        copy.wait()
    out[GAIN_ROW:PACKED, :] = rows.astype(BF16)


def unpack_kernel(got, frames, before, carry):
    for side in range(2):
        lanes = slice(side * LANES, (side + 1) * LANES)
        block = got[:, side * 32 : side * 32 + 32, :]
        frames[:, :, lanes] = block
        before[:, :, lanes] = block[8:16]
        for n in range(4):
            frame, col = n // 2, n % 2
            carry[frame, col * 16 : col * 16 + 16, lanes] = got[:, 64 + 4 * side + n, :]


def stack_kernel(*refs):
    bufs, out, sems = refs[:SECTIONS], refs[SECTIONS], refs[SECTIONS + 1]
    copies = []
    for which, buf in enumerate(bufs):
        to = out.at[pl.ds(which * PACKED, PACKED)]
        copies.append(pltpu.make_async_copy(buf, to, sems.at[which]))
        copies[-1].start()
    for copy in copies:
        copy.wait()


GROUPS = ((0, 3), (3, TAPS))


def base_of(section):
    rel = lax.rem(section - lax.axis_index("segment") + SECTIONS, SECTIONS)
    return pl.multiple_of(rel * PACKED, 16)


def fetch(section, bufs, out, terms, sems, gain_sem):
    core = core_of()
    base = base_of(section)
    gain_copy = pltpu.make_async_copy(bufs[0].at[pl.ds(base + GAIN_ROW, 16)], terms, gain_sem)
    gain_copy.start()
    copies = []
    for first, last in GROUPS:
        at, size = first * HALF, (last - first) * HALF
        for part in range(2):
            side = core if part == 0 else 1 - core
            src = bufs[part].at[pl.ds(pl.multiple_of(base + at, 16), size)]
            copies.append(
                pltpu.make_async_copy(src, out.at[side, pl.ds(at, size)], sems.at[len(copies)])
            )
            copies[-1].start()

    def wait(group):
        copies[2 * group].wait()
        copies[2 * group + 1].wait()

    def gain_row():
        gain_copy.wait()
        rows = terms[...].astype(F32)
        return rows[0:1] + (rows[1:2] + rows[2:3])

    return wait, gain_row


def times_taps(parts, weights, tap):
    rows = slice(tap * HALF, (tap + 3) * HALF)
    lhs = [part[:, side * HALF : (side + 1) * HALF] for side in range(2) for part in parts]
    taps = jnp.concatenate([weights[0, rows], weights[1, rows]], axis=0)
    return jnp.dot(jnp.concatenate(lhs, axis=-1), taps, preferred_element_type=F32)


def normed_of(values, gain_row):
    inverse = lax.rsqrt(jnp.mean(values * values, axis=-1, keepdims=True) + 1e-06)
    return (values * inverse * gain_row).astype(BF16)


def pieces(count, size):
    return [(at, min(size, count - at)) for at in range(0, count, size)]


def mix(source, weights, hidden, count, columns):
    rows = columns * 16
    for at, size in pieces(count, 4):
        parts = [source[at + k : at + k + size, 0:rows].reshape(size * rows, C) for k in range(3)]
        mixed = times_taps(parts, weights, 0)
        value = jax.nn.silu(mixed).astype(BF16).reshape(size, rows, C)
        for col in range(columns):
            hidden[col, at : at + size] = value[:, col * 16 : col * 16 + 16, :]


def spatial(hidden, weights, col, count):
    size = count * 16
    row = lax.broadcasted_iota(jnp.int32, (size, C), 0) % 16
    parts = [hidden[col + q, 0:count].reshape(size, C) for q in range(3)]
    y = [times_taps(parts, weights, 3 + 3 * p) for p in range(3)]
    down = jnp.where(row == 0, 0.0, pltpu.roll(y[0], 1, 0))
    up = jnp.where(row == 15, 0.0, pltpu.roll(y[2], size - 1, 0))
    return y[1] + down + up


def cols(col):
    return slice(col * 16, col * 16 + 16)


def pair_kernel(first, far, mid, left, right, stacked, swapped, *rest):
    if first:
        out, tails, tails_near = rest[:3]
    else:
        out, tail_out = rest[:2]
    weights, terms, sems, gain_sem, normed, hidden, second, normed2 = rest[-8:]
    bufs = (stacked, swapped)
    section = 0 if first else 2
    total = 24 if first else 20
    mine, shard = lax.axis_index("segment"), lax.axis_index("shard")
    shards = lax.axis_size("shard")
    loads = []
    for k in range(2):
        loads.append(
            fetch(section + k, bufs, weights.at[k], terms.at[k], sems.at[k], gain_sem.at[k])
        )
    last_gain = pltpu.make_async_copy(
        stacked.at[pl.ds(base_of(2) + GAIN_ROW, 16)], terms.at[2], gain_sem.at[2]
    )
    if first:
        last_gain.start()
    row = loads[0][1]()
    sources = (left, mid, right)
    for n, source in enumerate(sources):
        for at, size in pieces(total, 8):
            values = source[at : at + size].astype(F32).reshape(size * 32, C)
            normed[at : at + size, n * 32 : n * 32 + 32] = normed_of(values, row).reshape(size, 32, C)
    if first:
        tails[...] = normed[total - 2 : total, 32:64]

    @pl.when(mine == 0)
    def _():
        for n, source in enumerate(sources):
            normed[total - 18 : total - 16, n * 32 : n * 32 + 32] = source[total - 18 : total - 16]

    loads[0][0](0)
    count = total - 2
    mix(normed, weights.at[0], hidden, count, 6)
    loads[0][0](1)
    row = loads[1][1]()
    for col in range(4):
        source, at = ((left, cols(1)), (mid, cols(0)), (mid, cols(1)), (right, cols(0)))[col]
        a = source[2:, at, :].reshape(count * 16, C).astype(F32)
        result = (a + spatial(hidden, weights.at[0], col, count)).astype(BF16)
        if col in (1, 2):
            second[:, cols(col - 1), :] = result.reshape(count, 16, C)
        n = normed_of(result.astype(F32), row)
        if col == 0:
            n = jnp.where(shard == 0, jnp.zeros_like(n), n)
        if col == 3:
            n = jnp.where(shard == shards - 1, jnp.zeros_like(n), n)
        normed2[:, cols(col), :] = n.reshape(count, 16, C)
    own_tail = normed2[count - 2 : count, 16:48]
    if first:
        tails_near[0:2] = own_tail

    @pl.when(mine == 0)
    def _():
        for col in range(4):
            source, at = ((left, cols(1)), (mid, cols(0)), (mid, cols(1)), (right, cols(0)))[col]
            normed2[count - 18 : count - 16, cols(col)] = source[total - 20 : total - 18, at, :]

    loads[1][0](0)
    count = total - 4
    mix(normed2, weights.at[1], hidden, count, 4)
    loads[1][0](1)
    for col in range(2):
        a = second[2:, cols(col), :].reshape(count * 16, C).astype(F32)
        result = (a + spatial(hidden, weights.at[1], col, count)).astype(BF16).reshape(count, 16, C)
        if first:
            out[:, cols(col), :] = result
        else:
            for side in range(2):
                lanes = slice(side * LANES, (side + 1) * LANES)
                out[:, side * 32 + col * 16 : side * 32 + col * 16 + 16, :] = result[:, :, lanes]
    if first:
        last_gain.wait()
        rows = terms[2].astype(F32)
        row = rows[0:1] + (rows[1:2] + rows[2:3])
        last = out[count - 2 : count].astype(F32).reshape(64, C)
        tails_near[2:4] = normed_of(last, row).reshape(2, 32, C)

        @pl.when(mine == 0)
        def _():
            out[0:4] = far[...]

    else:
        tail_out[...] = own_tail


def place_kernel(_, own, came, wrapped, out):
    mine = lax.axis_index("segment")
    carry = jnp.where(mine == 2, came[2:4], wrapped[...])
    carry = jnp.where(mine == SECTIONS - 1, own[...], carry)
    for side in range(2):
        lanes = slice(side * LANES, (side + 1) * LANES)
        for n in range(4):
            out[:, 4 * side + n, :] = carry[n // 2, cols(n % 2), lanes]


def pair_call(first, far, sources, bufs):
    total = 24 if first else 20
    count = total - 2
    if first:
        outs = (shape_of(20, 32, C), shape_of(2, 32, C), shape_of(4, 32, C))
    else:
        outs = (shape_of(16, 72, LANES), shape_of(2, 32, C))
    return call(
        functools.partial(pair_kernel, first),
        outs,
        [VMEM] * 4 + [HBM] * 2,
        [
            pltpu.VMEM((2, 2, GAIN_ROW, C), BF16),
            pltpu.VMEM((3, 16, C), BF16),
            pltpu.SemaphoreType.DMA((2, 4)),
            pltpu.SemaphoreType.DMA((3,)),
            pltpu.VMEM((total, 96, C), BF16),
            pltpu.VMEM((6, count, 16, C), BF16),
            pltpu.VMEM((count, 32, C), BF16),
            pltpu.VMEM((count, 64, C), BF16),
        ],
        flops=1 << 31,
        moved=4 << 20,
    )(far, *sources, *bufs)


def place_call(out, own_tail, came, wrapped):
    rows = pl.BlockSpec((16, 8, LANES), lambda i: (0, 8, 0))

    def whole(array):
        return pl.BlockSpec(array.shape, lambda i: (0,) * array.ndim)

    return pl.pallas_call(
        place_kernel,
        out_shape=shape_of(16, 72, LANES),
        grid=(1,),
        in_specs=[pl.BlockSpec(memory_space=pl.ANY), whole(own_tail), whole(came), whole(wrapped)],
        out_specs=rows,
        input_output_aliases={0: 0},
        name="place",
        compiler_params=pltpu.CompilerParams(vmem_limit_bytes=16 << 20),
    )(out, own_tail, came, wrapped)


def join_kernel(frames, before, near, carry, out, both):
    out[8:24] = frames[...]
    out[0:8] = before[...]
    both[0:2] = near[...]
    both[2:4] = carry[...]

    @pl.when(lax.axis_index("segment") == 0)
    def _():
        out[4:6] = near[...]
        out[6:8] = carry[...]


def choose_kernel(own, came, out):
    out[...] = jnp.where(lax.axis_index("segment") == SECTIONS - 1, own[...], came[0:2])


def body(latents, norm_gain, time_weight, space_weight, carry_in):
    shards = lax.axis_size("shard")
    streams = lax.axis_size("stream")
    mine = lax.axis_index("segment")

    def ring(distance):
        return [(i, (i + distance) % SECTIONS) for i in range(SECTIONS)]

    def over_segments(array, pairs):
        return lax.ppermute(array, "segment", pairs)

    swap = [(i, i ^ 1) for i in range(streams)]
    up = [(i, i + 1) for i in range(shards - 1)]
    down = [(i + 1, i) for i in range(shards - 1)]

    block = lax.dynamic_index_in_dim(latents, mine, 0, keepdims=False)[0]
    chunks = call(chunk_kernel, shape_of(16, 72, LANES), [VMEM] * 2)(
        block.transpose(1, 0, 2), carry_in[0, :, 0]
    )
    got = lax.all_to_all(chunks, "shard", split_axis=0, concat_axis=0, tiled=True)

    packed = call(
        pack_kernel,
        shape_of(PACKED, C),
        [VMEM, HBM, HBM],
        [pltpu.SemaphoreType.DMA((TAPS,))],
        room=58,
    )(norm_gain, time_weight, space_weight)
    halves = [packed]
    for distance in (-1, 2, 1):
        halves.append(over_segments(packed, ring(distance)))
    stacked = call(
        stack_kernel,
        shape_of(SECTIONS * PACKED, C),
        [HBM] * SECTIONS,
        [pltpu.SemaphoreType.DMA((SECTIONS,))],
    )(*halves)
    bufs = (stacked, lax.ppermute(stacked, "stream", swap))

    frames, sent_before, carry = call(
        unpack_kernel, (shape_of(16, 32, C), shape_of(8, 32, C), shape_of(2, 32, C)), [VMEM]
    )(got)
    before = over_segments(sent_before, [(0, 1), (1, 2), (2, 3)])
    near = over_segments(carry, [(1, 0), (3, 2)])
    joined, both = call(join_kernel, (shape_of(24, 32, C), shape_of(4, 32, C)), [VMEM] * 4)(
        frames, before, near, carry
    )
    far = over_segments(both, [(2, 0)])

    def beside(array):
        came_left = lax.ppermute(array, "shard", up)
        came_right = lax.ppermute(array, "shard", down)
        return array, came_left, came_right

    middle, tail, tails_near = pair_call(True, far, beside(joined), bufs)
    sources = beside(middle)
    over = over_segments(tails_near, [(3, 2)])
    chosen = call(choose_kernel, shape_of(2, 32, C), [VMEM] * 2)(tail, over)
    wrapped = over_segments(chosen, [(3, 0), (2, 1)])
    out, own_tail = pair_call(False, over, sources, bufs)
    out = place_call(out, own_tail, over, wrapped)
    sent = lax.all_to_all(out, "shard", split_axis=0, concat_axis=0, tiled=True)
    main = jnp.concatenate([sent[:, 0:32], sent[:, 32:64]], axis=-1)
    decoded = main.reshape(32, 16, C).transpose(1, 0, 2)[None, None]
    kept_rows = jnp.concatenate([sent[:, 64:68], sent[:, 68:72]], axis=-1)
    carry_out = kept_rows.reshape(shards, 2, 2, C).transpose(1, 0, 2, 3).reshape(1, 2, 1, 32, C)
    return (decoded, carry_out)


def solution(mesh):
    placed = (
        P("stream", "shard", None, None, None),
        P("segment", None),
        P("segment", None, None, None),
        P("segment", None, None, None),
        P("segment", "stream", "shard", None, None),
    )
    return jax.shard_map(
        body,
        mesh=mesh,
        in_specs=placed,
        out_specs=(
            P(("stream", "segment"), "shard", None, None, None),
            P("segment", "stream", "shard", None, None),
        ),
        check_vma=False,
    )
```

```python
import functools

import jax
import jax.numpy as jnp
from jax import lax
from jax.experimental import pallas as pl
from jax.experimental.pallas import tpu as pltpu
from jax.sharding import PartitionSpec as P


C = 256
LANES = 128
HALF = 128
TAPS = 12
GAIN_ROW = TAPS * HALF
PACKED = GAIN_ROW + 16
SECTIONS = 4
F32 = jnp.float32
BF16 = jnp.bfloat16

VMEM = pl.BlockSpec(memory_space=pltpu.VMEM)
HBM = pl.BlockSpec(memory_space=pltpu.HBM)


def core_of():
    return lax.rem(lax.axis_index("stream"), 2)


def shape_of(*dims, dtype=BF16):
    return jax.ShapeDtypeStruct(dims, dtype)


def call(kernel, outs, in_specs, scratch=(), flops=1 << 20, moved=1 << 20, room=16):
    out_specs = tuple(VMEM for _ in outs) if isinstance(outs, tuple) else VMEM
    return pl.pallas_call(
        kernel,
        out_shape=outs,
        in_specs=in_specs,
        out_specs=out_specs,
        scratch_shapes=list(scratch),
        cost_estimate=pl.CostEstimate(flops=flops, bytes_accessed=moved, transcendentals=0),
        compiler_params=pltpu.CompilerParams(vmem_limit_bytes=room << 20),
    )


def chunk_kernel(columns, row, out):
    flat = columns[...].reshape(16, 32, C)
    for side in range(2):
        lanes = slice(side * LANES, (side + 1) * LANES)
        out[:, side * 32 : side * 32 + 32, :] = flat[:, :, lanes]
        for frame in range(2):
            at = 64 + 4 * side + 2 * frame
            for z in range(16):
                out[z, at : at + 2, :] = row[frame, 2 * z : 2 * z + 2, lanes]


def pack_kernel(gain, taps_time, taps_space, out, sems):
    at = pl.multiple_of(core_of() * HALF, HALF)
    copies = []
    for tap in range(TAPS):
        own = taps_time.at[0, tap] if tap < 3 else taps_space.at[0, tap - 3]
        copies.append(
            pltpu.make_async_copy(own.at[pl.ds(at, HALF)], out.at[pl.ds(tap * HALF, HALF)], sems.at[tap])
        )
        copies[-1].start()
    value = gain[...]
    high = value.astype(BF16)
    rest = value - high.astype(F32)
    middle = rest.astype(BF16)
    low = (rest - middle.astype(F32)).astype(BF16)
    pick = lax.broadcasted_iota(jnp.int32, (16, C), 0)
    rows = jnp.where(pick == 0, high.astype(F32), 0.0)
    rows = jnp.where(pick == 1, middle.astype(F32), rows)
    rows = jnp.where(pick == 2, low.astype(F32), rows)
    for copy in copies:
        copy.wait()
    out[GAIN_ROW:PACKED, :] = rows.astype(BF16)


def unpack_kernel(got, frames, before, carry):
    for side in range(2):
        lanes = slice(side * LANES, (side + 1) * LANES)
        block = got[:, side * 32 : side * 32 + 32, :]
        frames[:, :, lanes] = block
        before[:, :, lanes] = block[8:16]
        for n in range(4):
            frame, col = n // 2, n % 2
            carry[frame, col * 16 : col * 16 + 16, lanes] = got[:, 64 + 4 * side + n, :]


def stack_kernel(*refs):
    bufs, out, sems = refs[:SECTIONS], refs[SECTIONS], refs[SECTIONS + 1]
    copies = []
    for which, buf in enumerate(bufs):
        to = out.at[pl.ds(which * PACKED, PACKED)]
        copies.append(pltpu.make_async_copy(buf, to, sems.at[which]))
        copies[-1].start()
    for copy in copies:
        copy.wait()


GROUPS = ((0, 3), (3, TAPS))


def base_of(section):
    rel = lax.rem(section - lax.axis_index("segment") + SECTIONS, SECTIONS)
    return pl.multiple_of(rel * PACKED, 16)


def fetch(section, bufs, out, terms, sems, gain_sem):
    core = core_of()
    base = base_of(section)
    gain_copy = pltpu.make_async_copy(bufs[0].at[pl.ds(base + GAIN_ROW, 16)], terms, gain_sem)
    gain_copy.start()
    copies = []
    for first, last in GROUPS:
        at, size = first * HALF, (last - first) * HALF
        for part in range(2):
            side = core if part == 0 else 1 - core
            src = bufs[part].at[pl.ds(pl.multiple_of(base + at, 16), size)]
            copies.append(
                pltpu.make_async_copy(src, out.at[side, pl.ds(at, size)], sems.at[len(copies)])
            )
            copies[-1].start()

    def wait(group):
        copies[2 * group].wait()
        copies[2 * group + 1].wait()

    def gain_row():
        gain_copy.wait()
        rows = terms[...].astype(F32)
        return rows[0:1] + (rows[1:2] + rows[2:3])

    return wait, gain_row


def times_taps(parts, weights, tap):
    rows = slice(tap * HALF, (tap + 3) * HALF)
    lhs = [part[:, side * HALF : (side + 1) * HALF] for side in range(2) for part in parts]
    taps = jnp.concatenate([weights[0, rows], weights[1, rows]], axis=0)
    return jnp.dot(jnp.concatenate(lhs, axis=-1), taps, preferred_element_type=F32)


def normed_of(values, gain_row):
    inverse = lax.rsqrt(jnp.mean(values * values, axis=-1, keepdims=True) + 1e-06)
    return (values * inverse * gain_row).astype(BF16)


def pieces(count, size):
    return [(at, min(size, count - at)) for at in range(0, count, size)]


def mix(source, weights, hidden, count, columns):
    rows = columns * 16
    for at, size in pieces(count, 4):
        parts = [source[at + k : at + k + size, 0:rows].reshape(size * rows, C) for k in range(3)]
        mixed = times_taps(parts, weights, 0)
        value = jax.nn.silu(mixed).astype(BF16).reshape(size, rows, C)
        for col in range(columns):
            hidden[col, at : at + size] = value[:, col * 16 : col * 16 + 16, :]


def spatial(hidden, weights, col, count):
    size = count * 16
    row = lax.broadcasted_iota(jnp.int32, (size, C), 0) % 16
    parts = [hidden[col + q, 0:count].reshape(size, C) for q in range(3)]
    y = [times_taps(parts, weights, 3 + 3 * p) for p in range(3)]
    down = jnp.where(row == 0, 0.0, pltpu.roll(y[0], 1, 0))
    up = jnp.where(row == 15, 0.0, pltpu.roll(y[2], size - 1, 0))
    return y[1] + down + up


def cols(col):
    return slice(col * 16, col * 16 + 16)


def pair_kernel(first, mid, left, right, stacked, swapped, *rest):
    if first:
        out, tails, tails_near = rest[:3]
    else:
        out, tail_out = rest[:2]
    weights, terms, sems, gain_sem, normed, hidden, second, normed2 = rest[-8:]
    bufs = (stacked, swapped)
    section = 0 if first else 2
    total = 24 if first else 20
    mine, shard = lax.axis_index("segment"), lax.axis_index("shard")
    shards = lax.axis_size("shard")
    loads = []
    for k in range(2):
        loads.append(
            fetch(section + k, bufs, weights.at[k], terms.at[k], sems.at[k], gain_sem.at[k])
        )
    last_gain = pltpu.make_async_copy(
        stacked.at[pl.ds(base_of(2) + GAIN_ROW, 16)], terms.at[2], gain_sem.at[2]
    )
    if first:
        last_gain.start()
    row = loads[0][1]()
    sources = (left, mid, right)
    for n, source in enumerate(sources):
        for at, size in pieces(total, 8):
            values = source[at : at + size].astype(F32).reshape(size * 32, C)
            normed[at : at + size, n * 32 : n * 32 + 32] = normed_of(values, row).reshape(size, 32, C)
    if first:
        tails[...] = normed[total - 2 : total, 32:64]

    @pl.when(mine == 0)
    def _():
        for n, source in enumerate(sources):
            normed[total - 18 : total - 16, n * 32 : n * 32 + 32] = source[total - 18 : total - 16]

    loads[0][0](0)
    count = total - 2
    mix(normed, weights.at[0], hidden, count, 6)
    loads[0][0](1)
    row = loads[1][1]()
    for col in range(4):
        source, at = ((left, cols(1)), (mid, cols(0)), (mid, cols(1)), (right, cols(0)))[col]
        a = source[2:, at, :].reshape(count * 16, C).astype(F32)
        result = (a + spatial(hidden, weights.at[0], col, count)).astype(BF16)
        if col in (1, 2):
            second[:, cols(col - 1), :] = result.reshape(count, 16, C)
        n = normed_of(result.astype(F32), row)
        if col == 0:
            n = jnp.where(shard == 0, jnp.zeros_like(n), n)
        if col == 3:
            n = jnp.where(shard == shards - 1, jnp.zeros_like(n), n)
        normed2[:, cols(col), :] = n.reshape(count, 16, C)
    own_tail = normed2[count - 2 : count, 16:48]
    if first:
        tails_near[0:2] = own_tail

    @pl.when(mine == 0)
    def _():
        for col in range(4):
            source, at = ((left, cols(1)), (mid, cols(0)), (mid, cols(1)), (right, cols(0)))[col]
            normed2[count - 18 : count - 16, cols(col)] = source[total - 20 : total - 18, at, :]

    loads[1][0](0)
    count = total - 4
    mix(normed2, weights.at[1], hidden, count, 4)
    loads[1][0](1)
    for col in range(2):
        a = second[2:, cols(col), :].reshape(count * 16, C).astype(F32)
        result = (a + spatial(hidden, weights.at[1], col, count)).astype(BF16).reshape(count, 16, C)
        if first:
            out[:, cols(col), :] = result
        else:
            for side in range(2):
                lanes = slice(side * LANES, (side + 1) * LANES)
                out[:, side * 32 + col * 16 : side * 32 + col * 16 + 16, :] = result[:, :, lanes]
    if first:
        last_gain.wait()
        rows = terms[2].astype(F32)
        row = rows[0:1] + (rows[1:2] + rows[2:3])
        last = out[count - 2 : count].astype(F32).reshape(64, C)
        tails_near[2:4] = normed_of(last, row).reshape(2, 32, C)
    else:
        tail_out[...] = own_tail


def place_kernel(_, own, came, wrapped, out):
    mine = lax.axis_index("segment")
    carry = jnp.where(mine == 2, came[2:4], wrapped[...])
    carry = jnp.where(mine == SECTIONS - 1, own[...], carry)
    for side in range(2):
        lanes = slice(side * LANES, (side + 1) * LANES)
        for n in range(4):
            out[:, 4 * side + n, :] = carry[n // 2, cols(n % 2), lanes]


def pair_call(first, sources, bufs):
    total = 24 if first else 20
    count = total - 2
    if first:
        outs = (shape_of(20, 32, C), shape_of(2, 32, C), shape_of(4, 32, C))
    else:
        outs = (shape_of(16, 72, LANES), shape_of(2, 32, C))
    return call(
        functools.partial(pair_kernel, first),
        outs,
        [VMEM] * 3 + [HBM] * 2,
        [
            pltpu.VMEM((2, 2, GAIN_ROW, C), BF16),
            pltpu.VMEM((3, 16, C), BF16),
            pltpu.SemaphoreType.DMA((2, 4)),
            pltpu.SemaphoreType.DMA((3,)),
            pltpu.VMEM((total, 96, C), BF16),
            pltpu.VMEM((6, count, 16, C), BF16),
            pltpu.VMEM((count, 32, C), BF16),
            pltpu.VMEM((count, 64, C), BF16),
        ],
        flops=1 << 31,
        moved=4 << 20,
    )(*sources, *bufs)


def later_kernel(frames, far, out):
    out[...] = jnp.where(lax.axis_index("segment") == 0, far[...], frames[...])


def later_call(middle, far):
    rows = pl.BlockSpec((4, 32, C), lambda i: (0, 0, 0))
    return pl.pallas_call(
        later_kernel,
        out_shape=shape_of(20, 32, C),
        grid=(1,),
        in_specs=[rows, rows],
        out_specs=rows,
        input_output_aliases={0: 0},
        name="later",
        compiler_params=pltpu.CompilerParams(vmem_limit_bytes=16 << 20),
    )(middle, far)


def place_call(out, own_tail, came, wrapped):
    rows = pl.BlockSpec((16, 8, LANES), lambda i: (0, 8, 0))

    def whole(array):
        return pl.BlockSpec(array.shape, lambda i: (0,) * array.ndim)

    return pl.pallas_call(
        place_kernel,
        out_shape=shape_of(16, 72, LANES),
        grid=(1,),
        in_specs=[pl.BlockSpec(memory_space=pl.ANY), whole(own_tail), whole(came), whole(wrapped)],
        out_specs=rows,
        input_output_aliases={0: 0},
        name="place",
        compiler_params=pltpu.CompilerParams(vmem_limit_bytes=16 << 20),
    )(out, own_tail, came, wrapped)


def join_kernel(frames, before, near, carry, out, both):
    out[8:24] = frames[...]
    out[0:8] = before[...]
    both[0:2] = near[...]
    both[2:4] = carry[...]

    @pl.when(lax.axis_index("segment") == 0)
    def _():
        out[4:6] = near[...]
        out[6:8] = carry[...]


def choose_kernel(own, came, out):
    out[...] = jnp.where(lax.axis_index("segment") == SECTIONS - 1, own[...], came[0:2])


def body(latents, norm_gain, time_weight, space_weight, carry_in):
    shards = lax.axis_size("shard")
    streams = lax.axis_size("stream")
    mine = lax.axis_index("segment")

    def ring(distance):
        return [(i, (i + distance) % SECTIONS) for i in range(SECTIONS)]

    def over_segments(array, pairs):
        return lax.ppermute(array, "segment", pairs)

    swap = [(i, i ^ 1) for i in range(streams)]
    up = [(i, i + 1) for i in range(shards - 1)]
    down = [(i + 1, i) for i in range(shards - 1)]

    block = lax.dynamic_index_in_dim(latents, mine, 0, keepdims=False)[0]
    chunks = call(chunk_kernel, shape_of(16, 72, LANES), [VMEM] * 2)(
        block.transpose(1, 0, 2), carry_in[0, :, 0]
    )
    got = lax.all_to_all(chunks, "shard", split_axis=0, concat_axis=0, tiled=True)

    packed = call(
        pack_kernel,
        shape_of(PACKED, C),
        [VMEM, HBM, HBM],
        [pltpu.SemaphoreType.DMA((TAPS,))],
        room=58,
    )(norm_gain, time_weight, space_weight)
    halves = [packed]
    for distance in (-1, 2, 1):
        halves.append(over_segments(packed, ring(distance)))
    stacked = call(
        stack_kernel,
        shape_of(SECTIONS * PACKED, C),
        [HBM] * SECTIONS,
        [pltpu.SemaphoreType.DMA((SECTIONS,))],
    )(*halves)
    bufs = (stacked, lax.ppermute(stacked, "stream", swap))

    frames, sent_before, carry = call(
        unpack_kernel, (shape_of(16, 32, C), shape_of(8, 32, C), shape_of(2, 32, C)), [VMEM]
    )(got)
    before = over_segments(sent_before, [(0, 1), (1, 2), (2, 3)])
    near = over_segments(carry, [(1, 0), (3, 2)])
    joined, both = call(join_kernel, (shape_of(24, 32, C), shape_of(4, 32, C)), [VMEM] * 4)(
        frames, before, near, carry
    )
    far = over_segments(both, [(2, 0)])

    def beside(array):
        came_left = lax.ppermute(array, "shard", up)
        came_right = lax.ppermute(array, "shard", down)
        return array, came_left, came_right

    middle, tail, tails_near = pair_call(True, beside(joined), bufs)
    middle = later_call(middle, far)
    sources = beside(middle)
    over = over_segments(tails_near, [(3, 2)])
    chosen = call(choose_kernel, shape_of(2, 32, C), [VMEM] * 2)(tail, over)
    wrapped = over_segments(chosen, [(3, 0), (2, 1)])
    out, own_tail = pair_call(False, sources, bufs)
    out = place_call(out, own_tail, over, wrapped)
    sent = lax.all_to_all(out, "shard", split_axis=0, concat_axis=0, tiled=True)
    main = jnp.concatenate([sent[:, 0:32], sent[:, 32:64]], axis=-1)
    decoded = main.reshape(32, 16, C).transpose(1, 0, 2)[None, None]
    kept_rows = jnp.concatenate([sent[:, 64:68], sent[:, 68:72]], axis=-1)
    carry_out = kept_rows.reshape(shards, 2, 2, C).transpose(1, 0, 2, 3).reshape(1, 2, 1, 32, C)
    return (decoded, carry_out)


def solution(mesh):
    placed = (
        P("stream", "shard", None, None, None),
        P("segment", None),
        P("segment", None, None, None),
        P("segment", None, None, None),
        P("segment", "stream", "shard", None, None),
    )
    return jax.shard_map(
        body,
        mesh=mesh,
        in_specs=placed,
        out_specs=(
            P(("stream", "segment"), "shard", None, None, None),
            P("segment", "stream", "shard", None, None),
        ),
        check_vma=False,
    )
```
